32 devices in a mesh: section: 2 (over core), expert: 16 (over z, y, x).
Axes of the slice: x: 2, y: 2, z: 4, core: 2. Of those that a mesh axis runs over, the one named last changes fastest.
Arguments:
- fwd_states: bfloat16 [2, 2048, 2048], P('section', 'expert'), may hold values from -16 to 16
- fwd_routes: int32 [2, 2048, 2], P('section', 'expert'), may hold values from 0 to 15, all different within a row; in each aligned block of 128 rows (0 to 127, 128 to 255, ..., all dimensions but the last counted through in order) at most 20 rows name the same one
- bwd_states: bfloat16 [2, 2048, 2048], P('section', 'expert'), may hold values from -16 to 16
- bwd_routes: int32 [2, 2048, 2], P('section', 'expert'), may hold values from 0 to 15, all different within a row; in each aligned block of 128 rows (0 to 127, 128 to 255, ..., all dimensions but the last counted through in order) at most 20 rows name the same one
- bwd_cot: bfloat16 [2, 2048, 2048], P('section', 'expert'), may hold values from -1.5 to 1.5
- w_in: bfloat16 [16, 512, 2048], P('expert', 'section'), may hold values from -0.125 to 0.125
- w_out: bfloat16 [16, 512, 2048], P('expert', 'section'), may hold values from -0.25 to 0.25
Outputs:
- next_states: bfloat16 [2, 2048, 2048], P('section', 'expert')
- prev_cot: bfloat16 [2, 2048, 2048], P('section', 'expert')
- grad_w_in: float32 [16, 512, 2048], P('expert', 'section')
- grad_w_out: float32 [16, 512, 2048], P('expert', 'section')
The draws below stay inside these ranges and needn't reach their ends.
Inputs may be any that keep to these rules, and one draw needn't show every extreme that they name: `fwd_routes`: each row names 2 different experts; in each aligned block of 128 rows (the rows of one device in one section) no expert is named by more than 20 rows, and in some block one expert is named by exactly 20 rows. `bwd_routes`: each row names 2 different experts; in each aligned block of 128 rows (the rows of one device in one section) no expert is named by more than 20 rows, and in some block one expert is named by exactly 20 rows.
All inputs are finite; a program needn't handle non-finite values.
Results may differ from the reference program's by a relative error of at most 0.012.
Values may be sent and summed in bfloat16 or wider, within the bound.
A program may use at most 64 MiB of HBM per device.

```python
import math
import jax
import jax.numpy as jnp
import numpy as np
from jax import lax

D = 2048
H = 512
K = 2
TOK_DEV = 128
EXPERTS = 16
SECTIONS = 2
TOKENS = 2048
CAP = 20
N_EXPERT = 16


def draw_states(key, salt):
    key = jax.random.fold_in(key, salt)
    keys = jax.random.split(key, 3)
    full_shape = (SECTIONS, TOKENS, D)
    base = jax.random.normal(keys[0], full_shape, jnp.float32)
    row_scale = jnp.exp(jax.random.uniform(keys[1], (SECTIONS, TOKENS, 1), jnp.float32, math.log(0.3), math.log(3.0)))
    col_scale = jnp.exp(jax.random.uniform(keys[2], (1, 1, D), jnp.float32, math.log(0.3), math.log(3.0)))
    return jnp.clip(base * row_scale * col_scale, -16.0, 16.0).astype(jnp.bfloat16)


def draw_fwd_states(key, part):
    return draw_states(key, 11)


def draw_bwd_states(key, part):
    return draw_states(key, 23)


def shard_levels(own_key, dims, pieces, low, top_value):
    gain = 1.0
    for dim, parts in pieces:
        draws = jax.random.uniform(jax.random.fold_in(jax.random.fold_in(own_key, 6), dim), (parts,), jnp.float32, low / len(pieces), top_value / len(pieces))
        gain = gain * jnp.repeat(jnp.exp(draws), dims[dim] // parts).reshape((-1,) + (1,) * (len(dims) - 1 - dim))
    return gain


def deal_out(stream_key, own, number, rows, count, top, reach, slope):
    sequence = jax.random.permutation(stream_key, count)
    crowded, usual = portions_of(count, rows * top, reach, slope, True), portions_of(count, rows * top, reach, slope, False)
    places = jnp.arange(count)

    def named(sizes, turn):
        used = int((sizes > 0).sum())
        fixed = max(1, used // 4)
        passed = fixed + (places - fixed + turn * (used - fixed)) % max(1, count - fixed)
        return jnp.zeros((count,), jnp.int32).at[sequence[jnp.where(places < fixed, places, passed)]].set(jnp.asarray(sizes, jnp.int32))

    sizes = jnp.where(number % 4 == 0, named(crowded, number // 4), named(usual, number - number // 4 - 1))
    mixed = jax.random.permutation(jax.random.fold_in(own, 3), count)
    giver, taker = mixed[0:count // 2 * 2:2], mixed[1:count // 2 * 2:2]
    margin = jnp.minimum(sizes[giver] - 1, reach - sizes[taker]) // 2
    margin = jnp.where((giver == sequence[0]) | (taker == sequence[0]) | (sizes[taker] == 0), 0, jnp.maximum(margin, 0))
    passed = jax.random.randint(jax.random.fold_in(own, 4), (count // 2,), 0, 1 << 20) % (margin + 1)
    sizes = sizes.at[giver].add(-passed).at[taker].add(passed)
    members = jnp.searchsorted(jnp.cumsum(sizes), jnp.arange(rows * top), side="right").astype(jnp.int32)
    table = members.reshape(top, rows).T
    table = table[jax.random.permutation(jax.random.fold_in(own, 1), rows)]
    turn = jax.random.randint(jax.random.fold_in(own, 2), (rows, 1), 0, top)
    return jnp.take_along_axis(table, (jnp.arange(top)[None, :] + turn) % top, axis=1)


def portions_of(count, total, limit, lean, full):
    weights = [(1 << 20) // math.isqrt(standing ** lean) + 1 for standing in range(1, count + 1)]
    largest = limit if full else min(limit, max(-(-total // count), total * weights[0] // sum(weights)))
    least = 1 if total - largest >= count - 1 else 0
    holding, rest = [largest] + [least] * (count - 1), total - largest - least * (count - 1)
    while rest > 0:
        free = [i for i in range(1, count) if holding[i] < largest] or [i for i in range(1, count) if holding[i] < limit]
        pool, budget = sum([weights[i] for i in free]), rest
        for i in free:
            more = min(limit - holding[i], max(1, budget * weights[i] // pool), rest)
            holding[i] = holding[i] + more
            rest = rest - more
    return np.array(holding)


def scatter_about(stream_key, dims, scale, bound, cuts=(), kind=jnp.bfloat16):
    drawn = scale * jax.random.normal(stream_key, dims, jnp.float32)
    if cuts:
        drawn = drawn * shard_levels(stream_key, dims, cuts, -0.22, 0.18)
    return jnp.clip(drawn, -bound, bound).astype(kind)


def setup_inputs(seed: int = 0) -> dict:
    key_of = jax.random.split(jax.random.key(seed), 8)
    fwd_states = draw_fwd_states(jax.random.fold_in(key_of[7], 71), 0)
    fwd_routes_keys = jax.random.split(jax.random.fold_in(key_of[1], 1), SECTIONS * TOKENS // TOK_DEV)
    fwd_routes_turns = jax.random.permutation(jax.random.fold_in(key_of[1], 3), SECTIONS * TOKENS // TOK_DEV)
    fwd_routes = jax.vmap(lambda own, number: deal_out(jax.random.fold_in(key_of[1], 2), own, number, TOK_DEV, EXPERTS, K, CAP, 2))(fwd_routes_keys, fwd_routes_turns).reshape((SECTIONS, TOKENS, K))
    bwd_states = draw_bwd_states(jax.random.fold_in(key_of[7], 71), 0)
    bwd_routes_keys = jax.random.split(jax.random.fold_in(key_of[3], 1), SECTIONS * TOKENS // TOK_DEV)
    bwd_routes_turns = jax.random.permutation(jax.random.fold_in(key_of[3], 3), SECTIONS * TOKENS // TOK_DEV)
    bwd_routes = jax.vmap(lambda own, number: deal_out(jax.random.fold_in(key_of[3], 2), own, number, TOK_DEV, EXPERTS, K, CAP, 2))(bwd_routes_keys, bwd_routes_turns).reshape((SECTIONS, TOKENS, K))
    bwd_cot = scatter_about(key_of[4], (SECTIONS, TOKENS, D), 0.25, 1.5, ((0, 2), (1, 16)))
    w_in = scatter_about(key_of[5], (EXPERTS, H, D), D ** -0.5, 0.125, ((0, 16), (1, 2)))
    w_out = scatter_about(key_of[6], (EXPERTS, H, D), H ** -0.5, 0.25, ((0, 16), (1, 2)))
    return {"fwd_states": fwd_states, "fwd_routes": fwd_routes, "bwd_states": bwd_states, "bwd_routes": bwd_routes, "bwd_cot": bwd_cot, "w_in": w_in, "w_out": w_out}


EPSILON = 1e-06

def norm_rows(states):
    x_wide = states.astype(jnp.float32)
    inv_rms = lax.rsqrt(lax.optimization_barrier(jnp.mean(x_wide * x_wide, axis=-1, keepdims=True)) + EPSILON)
    return (x_wide, inv_rms, (x_wide * inv_rms).astype(jnp.bfloat16))

def contract_last(first_op, second_op):
    return lax.dot_general(first_op, second_op, (((1,), (1,)), ((), ())), preferred_element_type=jnp.float32)

def silu_slope(pre_act):
    sigma = jax.nn.sigmoid(pre_act)
    return sigma * (1.0 + pre_act * (1.0 - sigma))

def expert_table(expert_ids):
    flat_ids = expert_ids.reshape(-1).astype(jnp.int32)
    entries = flat_ids.shape[0]
    sorted_order = jnp.argsort(flat_ids, stable=True).astype(jnp.int32)
    ranked = flat_ids[sorted_order]
    starts = jnp.searchsorted(ranked, jnp.arange(EXPERTS, dtype=jnp.int32), side='left').astype(jnp.int32)
    rank_pos = jnp.arange(entries, dtype=jnp.int32) - starts[ranked]
    expert_depth = N_EXPERT * CAP
    row_table = jnp.full((EXPERTS * expert_depth,), entries, dtype=jnp.int32)
    row_table = row_table.at[ranked * expert_depth + rank_pos].set(sorted_order)
    return row_table.reshape(EXPERTS, expert_depth)

def spread_rows(values, top_count):
    zero_row = jnp.zeros((1, values.shape[-1]), values.dtype)
    return jnp.concatenate([jnp.repeat(values, top_count, axis=0), zero_row], axis=0)

def place_back(expert_outs, row_table, entries, top_count):
    placed = jnp.zeros((entries + 1, D), jnp.bfloat16).at[row_table.reshape(-1)].set(expert_outs.reshape(-1, D))
    picked = placed[:entries].reshape(-1, top_count, D).astype(jnp.float32)
    return lax.optimization_barrier(jnp.sum(picked, axis=1))

def forward_section(states, expert_ids, w_in, w_out):
    x_wide, inv_rms, normed = norm_rows(states)
    row_table = expert_table(expert_ids)
    top_count = expert_ids.shape[-1]
    spread = spread_rows(normed, top_count)

    def one_expert(operands):
        row_index, weight_in, weight_out = operands
        row_block = spread[row_index]
        hidden = jax.nn.silu(contract_last(row_block, weight_in)).astype(jnp.bfloat16)
        return jnp.dot(hidden, weight_out, preferred_element_type=jnp.float32).astype(jnp.bfloat16)
    expert_outs = lax.map(one_expert, (row_table, w_in, w_out))
    summed = place_back(expert_outs, row_table, spread.shape[0] - 1, top_count)
    return (x_wide + summed).astype(jnp.bfloat16)

def backward_section(states, expert_ids, cot, w_in, w_out):
    x_wide, inv_rms, normed = norm_rows(states)
    row_table = expert_table(expert_ids)
    top_count = expert_ids.shape[-1]
    spread_u = spread_rows(normed, top_count)
    spread_g = spread_rows(cot, top_count)

    def one_expert(operands):
        row_index, weight_in, weight_out = operands
        rows_u = spread_u[row_index]
        rows_g = spread_g[row_index]
        pre_act = contract_last(rows_u, weight_in)
        hidden = jax.nn.silu(pre_act).astype(jnp.bfloat16)
        grad_h = (contract_last(rows_g, weight_out) * silu_slope(pre_act)).astype(jnp.bfloat16)
        grad_u = jnp.dot(grad_h, weight_in, preferred_element_type=jnp.float32).astype(jnp.bfloat16)
        term_in = jnp.dot(grad_h.T, rows_u, preferred_element_type=jnp.float32).astype(jnp.bfloat16)
        term_out = jnp.dot(hidden.T, rows_g, preferred_element_type=jnp.float32).astype(jnp.bfloat16)
        return (grad_u, term_in, term_out)
    grad_u, term_in, term_out = lax.map(one_expert, (row_table, w_in, w_out))
    summed = place_back(grad_u, row_table, spread_u.shape[0] - 1, top_count)
    cot_wide = cot.astype(jnp.float32)
    cubed = inv_rms * inv_rms * inv_rms
    grad_x = cot_wide + inv_rms * summed - x_wide * cubed * lax.optimization_barrier(jnp.mean(summed * x_wide, axis=-1, keepdims=True))
    return (grad_x.astype(jnp.bfloat16), term_in, term_out)

def reference(fwd_states, fwd_routes, bwd_states, bwd_routes, bwd_cot, w_in, w_out):

    def forward_one(operands):
        return forward_section(operands[0], operands[1], w_in, w_out)
    outputs = lax.map(forward_one, (fwd_states, fwd_routes))

    def backward_one(totals, operands):
        grad_x, term_in, term_out = backward_section(operands[0], operands[1], operands[2], w_in, w_out)
        return ((totals[0] + term_in.astype(jnp.float32), totals[1] + term_out.astype(jnp.float32)), grad_x)
    empty_grad = jnp.zeros(w_in.shape, jnp.float32)
    (grad_in, grad_out), grads_x = lax.scan(backward_one, (empty_grad, empty_grad), (bwd_states, bwd_routes, bwd_cot))
    return (jnp.roll(outputs, 1, axis=0), jnp.roll(grads_x, -1, axis=0), grad_in, grad_out)
```

```python
import functools
import math
import jax
import jax.numpy as jnp
from jax import lax
from jax.experimental import pallas as pl
from jax.experimental.pallas import tpu as pltpu
from jax.sharding import PartitionSpec as P

EPSILON = 1e-06
CHUNKS = 4
ROWS = 16
F32, BF16 = jnp.float32, jnp.bfloat16
NT = (((1,), (1,)), ((), ()))
NN = (((1,), (0,)), ((), ()))
TN = (((0,), (0,)), ((), ()))
FWD, BWD, COT = 0, 1, 2


def mm(a, b, dims):
    return lax.dot_general(a, b, dims, preferred_element_type=F32)


def kernel(
    experts, sections, main, tail,
    xf_hbm, rf_hbm, xb_hbm, rb_hbm, g_hbm, win_hbm, wout_hbm,
    next_ref, prev_ref, gin_ref, gout_ref,
    xf_ref, rf_ref, xb_ref, rb_ref, g_ref,
    send, recv, home, back, u_tok, far_tok, far_routes, w_in, w_out, rows_u, rows_g, rows_f, act, slope, hid, side, front,
    tail_rows, part_in, part_out, table, spread, near_sum, far_send, far_part, result,
    loaded, tok_send, tok_recv, route_send, route_recv, near_send, near_recv, home_near, home_far, back_recv,
    cross_send, cross_recv, w_send, w_recv, p_send, p_recv, s_send, s_recv,
):
    tokens, depth = xf_hbm.shape
    wide = depth // CHUNKS
    blocks = main // ROWS
    q = ROWS // tail if tail else wide // 256
    thin = wide // q
    own_h = win_hbm.shape[0]
    near = experts // 2
    quarter = experts // 4
    span = near * ROWS
    n_main = experts * main
    me = lax.axis_index("expert")
    sec = lax.axis_index("section")
    half = me // near
    place = lax.rem(me, near)
    column = lax.rem(me, quarter)
    layer = place // quarter
    outward = jnp.where(half == 0, 1 - layer, layer)
    inner = outward == 0
    hub_layer = 1 + half
    my_relay = (2 - half) * quarter + column

    def source(r):
        return (2 - half + r * (1 - 2 * half)) * quarter + column

    def cols(c):
        return pl.ds(pl.multiple_of(c * wide, wide), wide)

    def strip(c, j):
        return pl.ds(pl.multiple_of(c * wide + j * thin, thin), thin)

    loads = [
        pltpu.make_async_copy(src, dst, loaded.at[i])
        for i, (src, dst) in enumerate(
            ((g_hbm, g_ref), (rb_hbm, rb_ref), (rf_hbm, rf_ref), (xb_hbm, xb_ref), (xf_hbm, xf_ref))
        )
    ]
    for load in loads:
        load.start()

    barrier = pltpu.get_barrier_semaphore()

    @pl.loop(1, near)
    def _(k):
        pl.semaphore_signal(barrier, inc=1, device_id={"expert": half * near + lax.rem(place + k, near)})

    @pl.loop(1, sections)
    def _(k):
        pl.semaphore_signal(barrier, inc=1, device_id={"section": lax.rem(sec + k, sections)})

    pl.semaphore_signal(barrier, inc=1, device_id={"expert": my_relay})

    @pl.when(inner)
    def _():
        pl.semaphore_signal(barrier, inc=1, device_id={"expert": source(1)})

    own_rows = pl.ds(pl.multiple_of(sec * own_h, own_h), own_h)
    weights = ((win_hbm, w_in), (wout_hbm, w_out))
    for i, (src, dst) in enumerate(weights):
        pltpu.make_async_copy(src, dst.at[own_rows], w_recv.at[i]).start()

    def routing(which, routes):
        lane_e = lax.broadcasted_iota(jnp.int32, (tokens, near), 1).astype(F32)
        row = lax.broadcasted_iota(jnp.int32, (tokens, tokens), 0)
        col = lax.broadcasted_iota(jnp.int32, (tokens, tokens), 1)
        names = (routes - half * near).astype(F32).astype(BF16)
        columns = mm((row == col).astype(F32).astype(BF16), names, NT)
        named = [columns[:, k : k + 1] for k in range(routes.shape[0])]
        hits = [(i == lane_e).astype(F32) for i in named]
        counts = functools.reduce(jnp.add, hits)
        rank = mm((row > col).astype(F32).astype(BF16), counts.astype(BF16), NN)
        spots = []
        for i, h in zip(named, hits):
            p = jnp.sum(h * rank, axis=1, keepdims=True)
            slot = jnp.full_like(p, -1.0)
            for b in range(blocks):
                low = b * ROWS
                slot = jnp.where((p >= low) & (p < low + ROWS), b * span + i * ROWS + (p - low), slot)
            spots.append((i, p, slot))
        lanes = table.shape[-1]
        lane = lax.broadcasted_iota(jnp.int32, (tokens, lanes), 1).astype(F32)
        for j in range(table.shape[1]):
            hit = jnp.zeros((tokens, lanes), F32)
            for i, p, slot in spots:
                if tail:
                    slot = jnp.where(p >= main, blocks * span + i * ROWS + j * tail + (p - main), slot)
                slot = jnp.where((i >= 0) & (i < near), slot, -1.0)
                hit = jnp.where(lane == slot, 1.0, hit)
            table[which, j] = hit.astype(BF16)

    def normalize(x_ref, which):
        @pl.loop(0, tokens // 16)
        def _(i):
            rows = pl.ds(pl.multiple_of(i * 16, 16), 16)
            x = x_ref[rows, :].astype(F32)
            inv = lax.rsqrt(jnp.mean(x * x, axis=-1, keepdims=True) + EPSILON)
            u_tok[which, rows, :] = (x * inv).astype(BF16)

    def picks(which, j):
        return table[which, j if tail else 0]

    def dispatch(stream, k, c, src):
        which = min(stream, 1) * 3 + k
        total = None
        for j in range(q):
            out = mm(picks(which, j), src[:, strip(c, j)], TN)
            for b in range(blocks):
                send[stream, k, :, c, :, b * wide + j * thin : b * wide + (j + 1) * thin] = (
                    out[b * span : (b + 1) * span].astype(BF16).reshape(near, ROWS, thin)
                )
            if tail:
                rest = out[blocks * span :]
                total = rest if total is None else total + rest
        if tail:
            send[stream, k, :, c, :, blocks * wide :] = total.astype(BF16).reshape(near, ROWS, thin)

    def to_near(stream, k, c, origin):
        pltpu.make_async_copy(
            send.at[stream, k, place, c], recv.at[stream, c, origin], near_recv.at[stream, c]
        ).start()

        @pl.loop(1, near)
        def _(i):
            spot = lax.rem(place + i, near)
            pltpu.make_async_remote_copy(
                src_ref=send.at[stream, k, spot, c],
                dst_ref=recv.at[stream, c, origin],
                send_sem=near_send.at[stream, k],
                recv_sem=near_recv.at[stream, c],
                device_id={"expert": half * near + spot},
            ).start()

    def own_tokens(stream, src):
        @pl.loop(0, CHUNKS)
        def _(c):
            dispatch(stream, 0, c, src)
            to_near(stream, 0, c, me)

    def to_relay(stream, src):
        @pl.loop(0, CHUNKS)
        def _(c):
            pltpu.make_async_remote_copy(
                src_ref=src.at[:, cols(c)], dst_ref=far_tok.at[stream, outward, :, cols(c)],
                send_sem=tok_send.at[stream], recv_sem=tok_recv.at[stream, outward, c],
                device_id={"expert": my_relay},
            ).start()

    def routes_to_relay(micro, src):
        pltpu.make_async_remote_copy(
            src_ref=src, dst_ref=far_routes.at[micro, outward],
            send_sem=route_send.at[micro], recv_sem=route_recv.at[micro, outward],
            device_id={"expert": my_relay},
        ).start()

    def relay_routes(micro):
        @pl.loop(0, 2)
        def _(r):
            mine = far_routes.at[micro, r]
            pltpu.make_async_copy(mine, mine, route_recv.at[micro, r]).wait()
            routing(micro * 3 + 1 + r, far_routes[micro, r])

    def relay(stream, r, low, high):
        @pl.loop(low, high)
        def _(c):
            block = far_tok.at[stream, r, :, cols(c)]
            pltpu.make_async_copy(block, block, tok_recv.at[stream, r, c]).wait()
            dispatch(stream, 1 + r, c, far_tok.at[stream, r])
            to_near(stream, 1 + r, c, source(r))

    def contract(stream, rows_ref, weight, total, low=0, high=CHUNKS):
        if low == 0:
            total[...] = jnp.zeros_like(total)

        @pl.loop(low, high)
        def _(c):
            buf = recv.at[stream, c]
            pltpu.make_async_copy(buf, buf, near_recv.at[stream, c]).wait()
            for b in range(blocks):
                rows_ref[b * experts * ROWS : (b + 1) * experts * ROWS, cols(c)] = buf[
                    :, :, b * wide : (b + 1) * wide
                ].reshape(experts * ROWS, wide)
            if tail:
                for h in range(2):
                    packed = buf[h * near : (h + 1) * near, :, blocks * wide :].reshape(span, thin)
                    for j in range(q):
                        rows_ref[n_main + h * near * tail : n_main + (h + 1) * near * tail, strip(c, j)] = mm(
                            spread[j], packed, NN
                        ).astype(BF16)
            total[...] += mm(rows_ref[:, cols(c)], weight[:, cols(c)], NT)

    def expand(act_rows, weight, slot):
        @pl.loop(0, CHUNKS)
        def _(c):
            buf = home.at[slot, c]
            step = min(512, wide)
            for i in range(wide // step):
                part = pl.ds(pl.multiple_of(c * wide + i * step, step), step)
                out = mm(act_rows[...], weight[:, part], NN).astype(BF16)
                for b in range(blocks):
                    buf[:, :, b * wide + i * step : b * wide + (i + 1) * step] = out[
                        b * experts * ROWS : (b + 1) * experts * ROWS
                    ].reshape(experts, ROWS, step)
                if tail:
                    tail_rows[:, i * step : (i + 1) * step] = out[n_main:]
            if tail:
                for h in range(2):
                    total = None
                    for j in range(q):
                        block = tail_rows[h * near * tail : (h + 1) * near * tail, j * thin : (j + 1) * thin]
                        moved = mm(spread[j], block, TN)
                        total = moved if total is None else total + moved
                    buf[h * near : (h + 1) * near, :, blocks * wide :] = total.astype(BF16).reshape(
                        near, ROWS, thin
                    )
            give_back(slot, c)

    def give_back(slot, c):
        for r in range(2):
            @pl.loop(0, quarter)
            def _(k):
                col = lax.rem(column + k, quarter)
                hub = hub_layer * quarter + col
                block = home.at[slot, c, (2 - half + r * (1 - 2 * half)) * quarter + col]
                there = back.at[slot, c, 1 + r, place]

                @pl.when(hub == me)
                def _():
                    pltpu.make_async_copy(block, there, back_recv.at[slot, c, 1 + r]).start()

                @pl.when(hub != me)
                def _():
                    pltpu.make_async_remote_copy(
                        src_ref=block, dst_ref=there,
                        send_sem=home_far.at[slot], recv_sem=back_recv.at[slot, c, 1 + r],
                        device_id={"expert": hub},
                    ).start()

        pltpu.make_async_copy(
            home.at[slot, c, me], back.at[slot, c, 0, place], back_recv.at[slot, c, 0]
        ).start()

        @pl.loop(1, near)
        def _(k):
            peer = half * near + lax.rem(place + k, near)
            pltpu.make_async_remote_copy(
                src_ref=home.at[slot, c, peer], dst_ref=back.at[slot, c, 0, place],
                send_sem=home_near.at[slot], recv_sem=back_recv.at[slot, c, 0],
                device_id={"expert": peer},
            ).start()

    def combine(slot, c, k, out_ref):
        buf = back.at[slot, c, k]
        pltpu.make_async_copy(buf, buf, back_recv.at[slot, c, k]).wait()
        for j in range(q):
            pieces = [
                buf[:, :, b * wide + j * thin : b * wide + (j + 1) * thin].reshape(span, thin) for b in range(blocks)
            ]
            if tail:
                pieces.append(buf[:, :, blocks * wide :].reshape(span, thin))
            out = mm(picks(slot * 3 + k, j), jnp.concatenate(pieces, axis=0), NN)
            out_ref[:, strip(c, j)] = out.astype(out_ref.dtype)

    def cross(slot, low, high):
        @pl.loop(low, high)
        def _(c):
            for r in (1, 0):
                combine(slot, c, 1 + r, far_send.at[slot, r])
                pltpu.make_async_remote_copy(
                    src_ref=far_send.at[slot, r, :, cols(c)], dst_ref=far_part.at[slot, :, cols(c)],
                    send_sem=cross_send.at[slot, r], recv_sem=cross_recv.at[slot, c],
                    device_id={"expert": source(r)},
                ).start()

    def own_sum(slot):
        @pl.loop(0, CHUNKS)
        def _(c):
            combine(slot, c, 0, near_sum.at[slot])

    def crossed(slot, c):
        block = far_part.at[slot, :, cols(c)]
        pltpu.make_async_copy(block, block, cross_recv.at[slot, c]).wait()

    def weight_terms(left, right, part):
        step = min(512, depth)

        @pl.loop(0, depth // step)
        def _(j):
            sl = pl.ds(pl.multiple_of(j * step, step), step)
            part[:, sl] = mm(left[...], right[:, sl], TN).astype(BF16)

    def share(i, part, out):
        pltpu.make_async_copy(part.at[own_rows], out.at[sec], p_recv.at[i]).start()

        @pl.loop(1, sections)
        def _(k):
            peer = lax.rem(sec + k, sections)
            pltpu.make_async_remote_copy(
                src_ref=part.at[pl.ds(pl.multiple_of(peer * own_h, own_h), own_h)],
                dst_ref=out.at[sec],
                send_sem=p_send.at[i], recv_sem=p_recv.at[i],
                device_id={"section": peer},
            ).start()

    outer = jnp.logical_not(inner)
    for load in loads[:3]:
        load.wait()
    pl.semaphore_wait(barrier, near + sections - 1 + jnp.where(inner, 1, 0))
    routes_to_relay(1, rb_ref)
    routes_to_relay(0, rf_ref)

    @pl.when(outer)
    def _():
        to_relay(COT, g_ref)

    for i, (src, dst) in enumerate(weights):
        @pl.loop(1, sections)
        def _(k):
            pltpu.make_async_remote_copy(
                src_ref=src, dst_ref=dst.at[own_rows],
                send_sem=w_send.at[i], recv_sem=w_recv.at[i],
                device_id={"section": lax.rem(sec + k, sections)},
            ).start()

    loads[3].wait()
    normalize(xb_ref, 1)

    @pl.when(outer)
    def _():
        to_relay(BWD, u_tok.at[1])

    @pl.when(inner)
    def _():
        to_relay(COT, g_ref)
        to_relay(BWD, u_tok.at[1])

    routing(3, rb_ref[...])
    own_tokens(COT, g_ref)
    own_tokens(BWD, u_tok.at[1])
    loads[4].wait()
    normalize(xf_ref, 0)
    routing(0, rf_ref[...])

    if tail:
        shape = (near * tail, span)
        row = lax.broadcasted_iota(jnp.int32, shape, 0).astype(F32)
        col = lax.broadcasted_iota(jnp.int32, shape, 1).astype(F32)
        start = row + jnp.floor((row + 0.5) * (1.0 / tail)) * (ROWS - tail)
        for j in range(q):
            spread[j] = jnp.where(col == start + j * tail, 1.0, 0.0).astype(BF16)

    for i, dst in enumerate((w_in, w_out)):
        pltpu.make_async_copy(dst, dst, w_recv.at[i]).wait()

    split = CHUNKS // 2
    last = CHUNKS - 1

    @pl.when(outer)
    def _():
        own_tokens(FWD, u_tok.at[0])

    @pl.when(inner)
    def _():
        to_relay(FWD, u_tok.at[0])
        relay_routes(1)
        relay(COT, 1, 0, CHUNKS)
        relay(BWD, 1, 0, CHUNKS)
        relay_routes(0)
        relay(COT, 0, 0, CHUNKS)
        relay(BWD, 0, 0, split)

    contract(COT, rows_g, w_out, slope)

    @pl.when(inner)
    def _():
        relay(BWD, 0, split, CHUNKS)
        own_tokens(FWD, u_tok.at[0])

    contract(BWD, rows_u, w_in, act, 0, last)

    @pl.when(outer)
    def _():
        to_relay(FWD, u_tok.at[0])

    contract(BWD, rows_u, w_in, act, last, CHUNKS)
    sigma = jax.nn.sigmoid(act[...])
    hid[...] = (slope[...] * (sigma * (1.0 + act[...] * (1.0 - sigma)))).astype(BF16)
    expand(hid, w_in, 1)
    side[...] = jax.nn.silu(act[...]).astype(BF16)

    @pl.when(inner)
    def _():
        relay(FWD, 1, 0, CHUNKS)
        relay(FWD, 0, 0, last)
        cross(1, 0, 1)
        relay(FWD, 0, last, CHUNKS)
        cross(1, 1, split)

    contract(FWD, rows_f, w_in, act)
    front[...] = jax.nn.silu(act[...]).astype(BF16)

    @pl.when(inner)
    def _():
        cross(1, split, last)

    expand(front, w_out, 0)

    @pl.when(inner)
    def _():
        cross(1, last, CHUNKS)

    weight_terms(hid, rows_u, part_in)
    share(0, part_in, gin_ref)
    weight_terms(side, rows_g, part_out)
    share(1, part_out, gout_ref)
    own_sum(1)

    @pl.when(inner)
    def _():
        cross(0, 0, CHUNKS)

    for c in range(CHUNKS):
        crossed(1, c)

    @pl.loop(0, tokens // 16)
    def _(i):
        rows = pl.ds(pl.multiple_of(i * 16, 16), 16)
        x = xb_ref[rows, :].astype(F32)
        total = near_sum[1, rows, :] + far_part[1, rows, :].astype(F32)
        inv = lax.rsqrt(jnp.mean(x * x, axis=-1, keepdims=True) + EPSILON)
        proj = jnp.mean(total * x, axis=-1, keepdims=True)
        grad = g_ref[rows, :].astype(F32) + inv * total - x * (inv * inv * inv) * proj
        result[1, rows, :] = grad.astype(BF16)

    to_prev = pltpu.make_async_remote_copy(
        src_ref=result.at[1], dst_ref=prev_ref, send_sem=s_send.at[1], recv_sem=s_recv.at[1],
        device_id={"section": lax.rem(sec + sections - 1, sections)},
    )
    to_prev.start()
    own_sum(0)

    @pl.loop(0, CHUNKS)
    def _(c):
        crossed(0, c)

        @pl.loop(0, tokens // 16)
        def _(i):
            rows = pl.ds(pl.multiple_of(i * 16, 16), 16)
            total = near_sum[0, rows, cols(c)] + far_part[0, rows, cols(c)].astype(F32)
            result[0, rows, cols(c)] = (xf_ref[rows, cols(c)].astype(F32) + total).astype(BF16)

        pltpu.make_async_remote_copy(
            src_ref=result.at[0, :, cols(c)], dst_ref=next_ref.at[:, cols(c)],
            send_sem=s_send.at[0], recv_sem=s_recv.at[0],
            device_id={"section": lax.rem(sec + 1, sections)},
        ).start()

    for i, (src, out) in enumerate(((win_hbm, gin_ref), (wout_hbm, gout_ref))):
        pltpu.make_async_copy(out, out, p_recv.at[i]).wait()

        @pl.loop(1, sections)
        def _(k):
            pltpu.make_async_copy(src, src, w_send.at[i]).wait()
            pltpu.make_async_copy(src, src, p_send.at[i]).wait()

    def drain(ref, sem):
        pltpu.make_async_copy(ref, ref, sem).wait()

    for stream in range(3):
        drain(g_ref, tok_send.at[stream])
        drain(send.at[0, 0, pl.ds(0, near - 1)], near_send.at[stream, 0])

    for micro, src in enumerate((rf_ref, rb_ref)):
        drain(src, route_send.at[micro])
    for slot in range(2):
        drain(home.at[0, :, pl.ds(0, near - 1)], home_near.at[slot])

    @pl.when(inner)
    def _():
        for stream in range(3):
            for r in range(2):
                drain(send.at[0, 0, pl.ds(0, near - 1)], near_send.at[stream, 1 + r])
        for slot in range(2):
            drain(home.at[0, :, pl.ds(0, near - 2)], home_far.at[slot])
            for r in range(2):
                drain(far_send.at[slot, r], cross_send.at[slot, r])

    @pl.when(jnp.logical_not(inner))
    def _():
        for slot in range(2):
            drain(home.at[0, :, pl.ds(0, near)], home_far.at[slot])

    to_prev.wait()
    drain(next_ref, s_recv.at[0])
    drain(result.at[0], s_send.at[0])


def per_device(fwd_states, fwd_routes, bwd_states, bwd_routes, bwd_cot, w_in, w_out):
    experts, sections = lax.axis_size("expert"), lax.axis_size("section")
    _, tokens, depth = fwd_states.shape
    top = fwd_routes.shape[2]
    own_h = w_in.shape[1]
    full_h = own_h * sections
    cap = max(2, (5 * tokens * top + 4 * experts - 1) // (4 * experts))
    main, tail = cap // ROWS * ROWS, cap % ROWS
    tail = next(t for t in (0, 2, 4, 8, 16) if t >= tail)
    main, tail = main + tail // ROWS * ROWS, tail % ROWS
    rows = experts * (main + tail)
    near = experts // 2
    wide = depth // CHUNKS
    q = ROWS // tail if tail else wide // 256
    thin = wide // q
    blocks = main // ROWS
    lanes = blocks * wide + (thin if tail else 0)
    picked = (blocks + (1 if tail else 0)) * near * ROWS
    buffers = [
        pltpu.VMEM((tokens, depth), BF16),
        pltpu.VMEM((top, tokens), jnp.int32),
        pltpu.VMEM((tokens, depth), BF16),
        pltpu.VMEM((top, tokens), jnp.int32),
        pltpu.VMEM((tokens, depth), BF16),
        pltpu.VMEM((3, 3, near, CHUNKS, ROWS, lanes), BF16),
        pltpu.VMEM((3, CHUNKS, experts, ROWS, lanes), BF16),
        pltpu.VMEM((2, CHUNKS, experts, ROWS, lanes), BF16),
        pltpu.VMEM((2, CHUNKS, 3, near, ROWS, lanes), BF16),
        pltpu.VMEM((2, tokens, depth), BF16),
        pltpu.VMEM((3, 2, tokens, depth), BF16),
        pltpu.VMEM((2, 2, top, tokens), jnp.int32),
        pltpu.VMEM((full_h, depth), BF16),
        pltpu.VMEM((full_h, depth), BF16),
        pltpu.VMEM((rows, depth), BF16),
        pltpu.VMEM((rows, depth), BF16),
        pltpu.VMEM((rows, depth), BF16),
        pltpu.VMEM((rows, full_h), F32),
        pltpu.VMEM((rows, full_h), F32),
        pltpu.VMEM((rows, full_h), BF16),
        pltpu.VMEM((rows, full_h), BF16),
        pltpu.VMEM((rows, full_h), BF16),
        pltpu.VMEM((max(ROWS, experts * tail), wide), BF16),
        pltpu.VMEM((full_h, depth), BF16),
        pltpu.VMEM((full_h, depth), BF16),
        pltpu.VMEM((6, q if tail else 1, tokens, picked), BF16),
        pltpu.VMEM((q, max(ROWS, near * tail), near * ROWS), BF16),
        pltpu.VMEM((2, tokens, depth), F32),
        pltpu.VMEM((2, 2, tokens, depth), BF16),
        pltpu.VMEM((2, tokens, depth), BF16),
        pltpu.VMEM((2, tokens, depth), BF16),
    ]
    grant = sum(math.prod(b.shape) * jnp.dtype(b.dtype).itemsize for b in buffers) + 3 * 1024 * 1024
    anywhere = pl.BlockSpec(memory_space=pl.ANY)
    dma = pltpu.SemaphoreType.DMA
    states = jax.ShapeDtypeStruct((tokens, depth), BF16)
    parts = jax.ShapeDtypeStruct((sections, own_h, depth), BF16)
    operands = (fwd_states[0], fwd_routes[0].T, bwd_states[0], bwd_routes[0].T, bwd_cot[0], w_in[0], w_out[0])
    next_states, prev_cot, part_in, part_out = pl.pallas_call(
        functools.partial(kernel, experts, sections, main, tail),
        out_shape=(states, states, parts, parts),
        in_specs=[pl.BlockSpec(memory_space=pltpu.HBM)] * 7,
        out_specs=(anywhere,) * 4,
        scratch_shapes=[
            *buffers,
            dma((5,)), dma((3,)), dma((3, 2, CHUNKS)), dma((2,)), dma((2, 2)), dma((3, 3)), dma((3, CHUNKS)),
            dma((2,)), dma((2,)), dma((2, CHUNKS, 3)), dma((2, 2)), dma((2, CHUNKS)),
            dma((2,)), dma((2,)), dma((2,)), dma((2,)), dma((2,)), dma((2,)),
        ],
        compiler_params=pltpu.CompilerParams(
            collective_id=0, has_side_effects=True, vmem_limit_bytes=grant
        ),
    )(*(pltpu.with_memory_space_constraint(v, pltpu.HBM) for v in operands))
    grad_in = jnp.sum(part_in.astype(F32), axis=0)
    grad_out = jnp.sum(part_out.astype(F32), axis=0)
    return next_states[None], prev_cot[None], grad_in[None], grad_out[None]


def solution(mesh):
    in_specs = (P("section", "expert", None),) * 5 + (P("expert", "section", None),) * 2
    out_specs = (P("section", "expert", None),) * 2 + (P("expert", "section", None),) * 2
    return jax.shard_map(
        per_device, mesh=mesh, in_specs=in_specs, out_specs=out_specs, check_vma=False
    )
```

```python
import functools
import math
import jax
import jax.numpy as jnp
from jax import lax
from jax.experimental import pallas as pl
from jax.experimental.pallas import tpu as pltpu
from jax.sharding import PartitionSpec as P

EPSILON = 1e-06
CHUNKS = 4
ROWS = 16
F32, BF16 = jnp.float32, jnp.bfloat16
NT = (((1,), (1,)), ((), ()))
NN = (((1,), (0,)), ((), ()))
TN = (((0,), (0,)), ((), ()))
FWD, BWD, COT = 0, 1, 2


def mm(a, b, dims):
    return lax.dot_general(a, b, dims, preferred_element_type=F32)


def kernel(
    experts, sections, main, tail,
    xf_hbm, rf_hbm, xb_hbm, rb_hbm, g_hbm, win_hbm, wout_hbm,
    next_ref, prev_ref, gin_ref, gout_ref,
    xf_ref, rf_ref, xb_ref, rb_ref, g_ref,
    send, recv, home, back, u_tok, far_tok, far_routes, w_in, w_out, rows_u, rows_g, rows_f, act, slope, hid, side, front,
    tail_rows, part_in, part_out, table, spread, near_sum, far_send, far_part, result,
    loaded, tok_send, tok_recv, route_send, route_recv, near_send, near_recv, home_near, home_far, back_recv,
    cross_send, cross_recv, w_send, w_recv, p_send, p_recv, s_send, s_recv,
):
    tokens, depth = xf_hbm.shape
    wide = depth // CHUNKS
    blocks = main // ROWS
    q = ROWS // tail if tail else wide // 256
    thin = wide // q
    own_h = win_hbm.shape[0]
    near = experts // 2
    quarter = experts // 4
    span = near * ROWS
    n_main = experts * main
    me = lax.axis_index("expert")
    sec = lax.axis_index("section")
    half = me // near
    place = lax.rem(me, near)
    column = lax.rem(me, quarter)
    layer = place // quarter
    outward = jnp.where(half == 0, 1 - layer, layer)
    inner = outward == 0
    hub_layer = 1 + half
    my_relay = (2 - half) * quarter + column

    def source(r):
        return (2 - half + r * (1 - 2 * half)) * quarter + column

    def cols(c):
        return pl.ds(pl.multiple_of(c * wide, wide), wide)

    def strip(c, j):
        return pl.ds(pl.multiple_of(c * wide + j * thin, thin), thin)

    loads = [
        pltpu.make_async_copy(src, dst, loaded.at[i])
        for i, (src, dst) in enumerate(
            ((g_hbm, g_ref), (rb_hbm, rb_ref), (rf_hbm, rf_ref), (xb_hbm, xb_ref), (xf_hbm, xf_ref))
        )
    ]
    for load in loads:
        load.start()

    barrier = pltpu.get_barrier_semaphore()

    @pl.loop(1, near)
    def _(k):
        pl.semaphore_signal(barrier, inc=1, device_id={"expert": half * near + lax.rem(place + k, near)})

    @pl.loop(1, sections)
    def _(k):
        pl.semaphore_signal(barrier, inc=1, device_id={"section": lax.rem(sec + k, sections)})

    pl.semaphore_signal(barrier, inc=1, device_id={"expert": my_relay})

    @pl.when(inner)
    def _():
        pl.semaphore_signal(barrier, inc=1, device_id={"expert": source(1)})

    own_rows = pl.ds(pl.multiple_of(sec * own_h, own_h), own_h)

    def routing(which, routes):
        lane_e = lax.broadcasted_iota(jnp.int32, (tokens, near), 1).astype(F32)
        row = lax.broadcasted_iota(jnp.int32, (tokens, tokens), 0)
        col = lax.broadcasted_iota(jnp.int32, (tokens, tokens), 1)
        names = (routes - half * near).astype(F32).astype(BF16)
        columns = mm((row == col).astype(F32).astype(BF16), names, NT)
        named = [columns[:, k : k + 1] for k in range(routes.shape[0])]
        hits = [(i == lane_e).astype(F32) for i in named]
        counts = functools.reduce(jnp.add, hits)
        rank = mm((row > col).astype(F32).astype(BF16), counts.astype(BF16), NN)
        spots = []
        for i, h in zip(named, hits):
            p = jnp.sum(h * rank, axis=1, keepdims=True)
            slot = jnp.full_like(p, -1.0)
            for b in range(blocks):
                low = b * ROWS
                slot = jnp.where((p >= low) & (p < low + ROWS), b * span + i * ROWS + (p - low), slot)
            spots.append((i, p, slot))
        lanes = table.shape[-1]
        lane = lax.broadcasted_iota(jnp.int32, (tokens, lanes), 1).astype(F32)
        for j in range(table.shape[1]):
            hit = jnp.zeros((tokens, lanes), F32)
            for i, p, slot in spots:
                if tail:
                    slot = jnp.where(p >= main, blocks * span + i * ROWS + j * tail + (p - main), slot)
                slot = jnp.where((i >= 0) & (i < near), slot, -1.0)
                hit = jnp.where(lane == slot, 1.0, hit)
            table[which, j] = hit.astype(BF16)

    def normalize(x_ref, which):
        @pl.loop(0, tokens // 16)
        def _(i):
            rows = pl.ds(pl.multiple_of(i * 16, 16), 16)
            x = x_ref[rows, :].astype(F32)
            inv = lax.rsqrt(jnp.mean(x * x, axis=-1, keepdims=True) + EPSILON)
            u_tok[which, rows, :] = (x * inv).astype(BF16)

    def picks(which, j):
        return table[which, j if tail else 0]

    def dispatch(stream, k, c, src):
        which = min(stream, 1) * 3 + k
        total = None
        for j in range(q):
            out = mm(picks(which, j), src[:, strip(c, j)], TN)
            for b in range(blocks):
                send[stream, k, :, c, :, b * wide + j * thin : b * wide + (j + 1) * thin] = (
                    out[b * span : (b + 1) * span].astype(BF16).reshape(near, ROWS, thin)
                )
            if tail:
                rest = out[blocks * span :]
                total = rest if total is None else total + rest
        if tail:
            send[stream, k, :, c, :, blocks * wide :] = total.astype(BF16).reshape(near, ROWS, thin)

    def to_near(stream, k, c, origin):
        pltpu.make_async_copy(
            send.at[stream, k, place, c], recv.at[stream, c, origin], near_recv.at[stream, c]
        ).start()

        @pl.loop(1, near)
        def _(i):
            spot = lax.rem(place + i, near)
            pltpu.make_async_remote_copy(
                src_ref=send.at[stream, k, spot, c],
                dst_ref=recv.at[stream, c, origin],
                send_sem=near_send.at[stream, k],
                recv_sem=near_recv.at[stream, c],
                device_id={"expert": half * near + spot},
            ).start()

    def own_tokens(stream, src):
        @pl.loop(0, CHUNKS)
        def _(c):
            dispatch(stream, 0, c, src)
            to_near(stream, 0, c, me)

    def to_relay(stream, src):
        @pl.loop(0, CHUNKS)
        def _(c):
            pltpu.make_async_remote_copy(
                src_ref=src.at[:, cols(c)], dst_ref=far_tok.at[stream, outward, :, cols(c)],
                send_sem=tok_send.at[stream], recv_sem=tok_recv.at[stream, outward, c],
                device_id={"expert": my_relay},
            ).start()

    def routes_to_relay(micro, src):
        pltpu.make_async_remote_copy(
            src_ref=src, dst_ref=far_routes.at[micro, outward],
            send_sem=route_send.at[micro], recv_sem=route_recv.at[micro, outward],
            device_id={"expert": my_relay},
        ).start()

    def relay_routes(micro):
        @pl.loop(0, 2)
        def _(r):
            mine = far_routes.at[micro, r]
            pltpu.make_async_copy(mine, mine, route_recv.at[micro, r]).wait()
            routing(micro * 3 + 1 + r, far_routes[micro, r])

    def relay(stream, r, low, high):
        @pl.loop(low, high)
        def _(c):
            block = far_tok.at[stream, r, :, cols(c)]
            pltpu.make_async_copy(block, block, tok_recv.at[stream, r, c]).wait()
            dispatch(stream, 1 + r, c, far_tok.at[stream, r])
            to_near(stream, 1 + r, c, source(r))

    def contract(stream, rows_ref, weight, total, low=0, high=CHUNKS):
        if low == 0:
            total[...] = jnp.zeros_like(total)

        @pl.loop(low, high)
        def _(c):
            buf = recv.at[stream, c]
            pltpu.make_async_copy(buf, buf, near_recv.at[stream, c]).wait()
            for b in range(blocks):
                rows_ref[b * experts * ROWS : (b + 1) * experts * ROWS, cols(c)] = buf[
                    :, :, b * wide : (b + 1) * wide
                ].reshape(experts * ROWS, wide)
            if tail:
                for h in range(2):
                    packed = buf[h * near : (h + 1) * near, :, blocks * wide :].reshape(span, thin)
                    for j in range(q):
                        rows_ref[n_main + h * near * tail : n_main + (h + 1) * near * tail, strip(c, j)] = mm(
                            spread[j], packed, NN
                        ).astype(BF16)
            total[...] += mm(rows_ref[:, cols(c)], weight[:, cols(c)], NT)

    def expand(act_rows, weight, slot):
        @pl.loop(0, CHUNKS)
        def _(c):
            buf = home.at[slot, c]
            step = min(512, wide)
            for i in range(wide // step):
                part = pl.ds(pl.multiple_of(c * wide + i * step, step), step)
                out = mm(act_rows[...], weight[:, part], NN).astype(BF16)
                for b in range(blocks):
                    buf[:, :, b * wide + i * step : b * wide + (i + 1) * step] = out[
                        b * experts * ROWS : (b + 1) * experts * ROWS
                    ].reshape(experts, ROWS, step)
                if tail:
                    tail_rows[:, i * step : (i + 1) * step] = out[n_main:]
            if tail:
                for h in range(2):
                    total = None
                    for j in range(q):
                        block = tail_rows[h * near * tail : (h + 1) * near * tail, j * thin : (j + 1) * thin]
                        moved = mm(spread[j], block, TN)
                        total = moved if total is None else total + moved
                    buf[h * near : (h + 1) * near, :, blocks * wide :] = total.astype(BF16).reshape(
                        near, ROWS, thin
                    )
            give_far(slot, c)

    def give_far(slot, c):
        for r in range(2):
            @pl.loop(0, quarter)
            def _(k):
                col = lax.rem(column + k, quarter)
                hub = hub_layer * quarter + col
                block = home.at[slot, c, (2 - half + r * (1 - 2 * half)) * quarter + col]
                there = back.at[slot, c, 1 + r, place]

                @pl.when(hub == me)
                def _():
                    pltpu.make_async_copy(block, there, back_recv.at[slot, c, 1 + r]).start()

                @pl.when(hub != me)
                def _():
                    pltpu.make_async_remote_copy(
                        src_ref=block, dst_ref=there,
                        send_sem=home_far.at[slot], recv_sem=back_recv.at[slot, c, 1 + r],
                        device_id={"expert": hub},
                    ).start()

    def give_near(slot):
        @pl.loop(0, CHUNKS)
        def _(c):
            pltpu.make_async_copy(
                home.at[slot, c, me], back.at[slot, c, 0, place], back_recv.at[slot, c, 0]
            ).start()

            @pl.loop(1, near)
            def _(k):
                peer = half * near + lax.rem(place + k, near)
                pltpu.make_async_remote_copy(
                    src_ref=home.at[slot, c, peer], dst_ref=back.at[slot, c, 0, place],
                    send_sem=home_near.at[slot], recv_sem=back_recv.at[slot, c, 0],
                    device_id={"expert": peer},
                ).start()

    def combine(slot, c, k, out_ref):
        buf = back.at[slot, c, k]
        pltpu.make_async_copy(buf, buf, back_recv.at[slot, c, k]).wait()
        for j in range(q):
            pieces = [
                buf[:, :, b * wide + j * thin : b * wide + (j + 1) * thin].reshape(span, thin) for b in range(blocks)
            ]
            if tail:
                pieces.append(buf[:, :, blocks * wide :].reshape(span, thin))
            out = mm(picks(slot * 3 + k, j), jnp.concatenate(pieces, axis=0), NN)
            out_ref[:, strip(c, j)] = out.astype(out_ref.dtype)

    def cross(slot, c, r):
        combine(slot, c, 1 + r, far_send.at[slot, r])
        pltpu.make_async_remote_copy(
            src_ref=far_send.at[slot, r, :, cols(c)], dst_ref=far_part.at[slot, :, cols(c)],
            send_sem=cross_send.at[slot, r], recv_sem=cross_recv.at[slot, c],
            device_id={"expert": source(r)},
        ).start()

    def cross_range(slot, r, low, high):
        @pl.loop(low, high)
        def _(c):
            cross(slot, c, r)

    def own_sum(slot):
        @pl.loop(0, CHUNKS)
        def _(c):
            combine(slot, c, 0, near_sum.at[slot])

    def crossed(slot, c):
        block = far_part.at[slot, :, cols(c)]
        pltpu.make_async_copy(block, block, cross_recv.at[slot, c]).wait()

    def weight_terms(left, right, part):
        step = min(512, depth)

        @pl.loop(0, depth // step)
        def _(j):
            sl = pl.ds(pl.multiple_of(j * step, step), step)
            part[:, sl] = mm(left[...], right[:, sl], TN).astype(BF16)

    def share(i, part, out):
        pltpu.make_async_copy(part.at[own_rows], out.at[sec], p_recv.at[i]).start()

        @pl.loop(1, sections)
        def _(k):
            peer = lax.rem(sec + k, sections)
            pltpu.make_async_remote_copy(
                src_ref=part.at[pl.ds(pl.multiple_of(peer * own_h, own_h), own_h)],
                dst_ref=out.at[sec],
                send_sem=p_send.at[i], recv_sem=p_recv.at[i],
                device_id={"section": peer},
            ).start()

    outer = jnp.logical_not(inner)
    for load in loads[:3]:
        load.wait()
    pl.semaphore_wait(barrier, near + sections - 1 + jnp.where(inner, 1, 0))
    routes_to_relay(1, rb_ref)
    routes_to_relay(0, rf_ref)

    @pl.when(outer)
    def _():
        to_relay(COT, g_ref)

    loads[3].wait()
    normalize(xb_ref, 1)

    @pl.when(outer)
    def _():
        to_relay(BWD, u_tok.at[1])

    @pl.when(inner)
    def _():
        to_relay(COT, g_ref)
        to_relay(BWD, u_tok.at[1])

    routing(3, rb_ref[...])
    own_tokens(COT, g_ref)
    own_tokens(BWD, u_tok.at[1])
    loads[4].wait()
    normalize(xf_ref, 0)
    routing(0, rf_ref[...])

    for i, (src, dst) in enumerate(((win_hbm, w_in), (wout_hbm, w_out))):
        pltpu.make_async_copy(src, dst.at[own_rows], w_recv.at[i]).start()

        @pl.loop(1, sections)
        def _(k):
            pltpu.make_async_remote_copy(
                src_ref=src, dst_ref=dst.at[own_rows],
                send_sem=w_send.at[i], recv_sem=w_recv.at[i],
                device_id={"section": lax.rem(sec + k, sections)},
            ).start()

    if tail:
        shape = (near * tail, span)
        row = lax.broadcasted_iota(jnp.int32, shape, 0).astype(F32)
        col = lax.broadcasted_iota(jnp.int32, shape, 1).astype(F32)
        start = row + jnp.floor((row + 0.5) * (1.0 / tail)) * (ROWS - tail)
        for j in range(q):
            spread[j] = jnp.where(col == start + j * tail, 1.0, 0.0).astype(BF16)

    split = CHUNKS // 2
    last = CHUNKS - 1

    @pl.when(outer)
    def _():
        own_tokens(FWD, u_tok.at[0])

    @pl.when(inner)
    def _():
        to_relay(FWD, u_tok.at[0])
        relay_routes(1)
        relay(COT, 1, 0, CHUNKS)
        relay(BWD, 1, 0, CHUNKS)
        relay_routes(0)
        relay(COT, 0, 0, CHUNKS)
        relay(BWD, 0, 0, split)

    for i, dst in enumerate((w_in, w_out)):
        pltpu.make_async_copy(dst, dst, w_recv.at[i]).wait()

    contract(COT, rows_g, w_out, slope)

    @pl.when(inner)
    def _():
        relay(BWD, 0, split, CHUNKS)
        own_tokens(FWD, u_tok.at[0])

    contract(BWD, rows_u, w_in, act, 0, last)

    @pl.when(outer)
    def _():
        to_relay(FWD, u_tok.at[0])

    contract(BWD, rows_u, w_in, act, last, CHUNKS)
    sigma = jax.nn.sigmoid(act[...])
    hid[...] = (slope[...] * (sigma * (1.0 + act[...] * (1.0 - sigma)))).astype(BF16)
    expand(hid, w_in, 1)
    side[...] = jax.nn.silu(act[...]).astype(BF16)

    @pl.when(inner)
    def _():
        relay(FWD, 1, 0, CHUNKS)
        relay(FWD, 0, 0, last)
        cross_range(1, 0, 0, 1)
        relay(FWD, 0, last, CHUNKS)
        give_near(1)
        cross_range(1, 0, 1, CHUNKS)

    @pl.when(outer)
    def _():
        give_near(1)

    contract(FWD, rows_f, w_in, act)
    front[...] = jax.nn.silu(act[...]).astype(BF16)

    @pl.when(inner)
    def _():
        cross_range(1, 1, 0, split)

    expand(front, w_out, 0)
    give_near(0)

    @pl.when(inner)
    def _():
        cross_range(1, 1, split, CHUNKS)

    weight_terms(hid, rows_u, part_in)
    share(0, part_in, gin_ref)
    weight_terms(side, rows_g, part_out)
    share(1, part_out, gout_ref)
    own_sum(1)

    @pl.when(inner)
    def _():
        @pl.loop(0, CHUNKS)
        def _(c):
            cross(0, c, 1)
            cross(0, c, 0)

    for c in range(CHUNKS):
        crossed(1, c)

    @pl.loop(0, tokens // 16)
    def _(i):
        rows = pl.ds(pl.multiple_of(i * 16, 16), 16)
        x = xb_ref[rows, :].astype(F32)
        total = near_sum[1, rows, :] + far_part[1, rows, :].astype(F32)
        inv = lax.rsqrt(jnp.mean(x * x, axis=-1, keepdims=True) + EPSILON)
        proj = jnp.mean(total * x, axis=-1, keepdims=True)
        grad = g_ref[rows, :].astype(F32) + inv * total - x * (inv * inv * inv) * proj
        result[1, rows, :] = grad.astype(BF16)

    to_prev = pltpu.make_async_remote_copy(
        src_ref=result.at[1], dst_ref=prev_ref, send_sem=s_send.at[1], recv_sem=s_recv.at[1],
        device_id={"section": lax.rem(sec + sections - 1, sections)},
    )
    to_prev.start()
    own_sum(0)

    @pl.loop(0, CHUNKS)
    def _(c):
        crossed(0, c)

        @pl.loop(0, tokens // 16)
        def _(i):
            rows = pl.ds(pl.multiple_of(i * 16, 16), 16)
            total = near_sum[0, rows, cols(c)] + far_part[0, rows, cols(c)].astype(F32)
            result[0, rows, cols(c)] = (xf_ref[rows, cols(c)].astype(F32) + total).astype(BF16)

        pltpu.make_async_remote_copy(
            src_ref=result.at[0, :, cols(c)], dst_ref=next_ref.at[:, cols(c)],
            send_sem=s_send.at[0], recv_sem=s_recv.at[0],
            device_id={"section": lax.rem(sec + 1, sections)},
        ).start()

    for i, (src, out) in enumerate(((win_hbm, gin_ref), (wout_hbm, gout_ref))):
        pltpu.make_async_copy(out, out, p_recv.at[i]).wait()

        @pl.loop(1, sections)
        def _(k):
            pltpu.make_async_copy(src, src, w_send.at[i]).wait()
            pltpu.make_async_copy(src, src, p_send.at[i]).wait()

    def drain(ref, sem):
        pltpu.make_async_copy(ref, ref, sem).wait()

    for stream in range(3):
        drain(g_ref, tok_send.at[stream])
        drain(send.at[0, 0, pl.ds(0, near - 1)], near_send.at[stream, 0])

    for micro, src in enumerate((rf_ref, rb_ref)):
        drain(src, route_send.at[micro])
    for slot in range(2):
        drain(home.at[0, :, pl.ds(0, near - 1)], home_near.at[slot])

    @pl.when(inner)
    def _():
        for stream in range(3):
            for r in range(2):
                drain(send.at[0, 0, pl.ds(0, near - 1)], near_send.at[stream, 1 + r])
        for slot in range(2):
            drain(home.at[0, :, pl.ds(0, near - 2)], home_far.at[slot])
            for r in range(2):
                drain(far_send.at[slot, r], cross_send.at[slot, r])

    @pl.when(jnp.logical_not(inner))
    def _():
        for slot in range(2):
            drain(home.at[0, :, pl.ds(0, near)], home_far.at[slot])

    to_prev.wait()
    drain(next_ref, s_recv.at[0])
    drain(result.at[0], s_send.at[0])


def finish(next_ref, prev_ref, pin_ref, pout_ref, next_out, prev_out, gin_out, gout_out, sum_in, sum_out, sems):
    own_h = sum_in.shape[0]
    step = own_h // 4
    moves = [
        pltpu.make_async_copy(next_ref, next_out, sems.at[0]),
        pltpu.make_async_copy(prev_ref, prev_out, sems.at[1]),
    ]
    for move in moves:
        move.start()
    for i, (part, total, out) in enumerate(((pin_ref, sum_in, gin_out), (pout_ref, sum_out, gout_out))):
        @pl.loop(0, own_h // step)
        def _(b):
            @pl.loop(0, step // 16)
            def _(j):
                rows = pl.ds(pl.multiple_of(b * step + j * 16, 16), 16)
                total[rows, :] = functools.reduce(
                    jnp.add, [part[k, rows, :].astype(F32) for k in range(part.shape[0])]
                )

            block = pl.ds(pl.multiple_of(b * step, step), step)
            pltpu.make_async_copy(total.at[block], out.at[block], sems.at[2 + i]).start()

    for move in moves:
        move.wait()
    for i, (total, out) in enumerate(((sum_in, gin_out), (sum_out, gout_out))):
        pltpu.make_async_copy(total, out, sems.at[2 + i]).wait()


def per_device(fwd_states, fwd_routes, bwd_states, bwd_routes, bwd_cot, w_in, w_out):
    experts, sections = lax.axis_size("expert"), lax.axis_size("section")
    _, tokens, depth = fwd_states.shape
    top = fwd_routes.shape[2]
    own_h = w_in.shape[1]
    full_h = own_h * sections
    cap = max(2, (5 * tokens * top + 4 * experts - 1) // (4 * experts))
    main, tail = cap // ROWS * ROWS, cap % ROWS
    tail = next(t for t in (0, 2, 4, 8, 16) if t >= tail)
    main, tail = main + tail // ROWS * ROWS, tail % ROWS
    rows = experts * (main + tail)
    near = experts // 2
    wide = depth // CHUNKS
    q = ROWS // tail if tail else wide // 256
    thin = wide // q
    blocks = main // ROWS
    lanes = blocks * wide + (thin if tail else 0)
    picked = (blocks + (1 if tail else 0)) * near * ROWS
    buffers = [
        pltpu.VMEM((tokens, depth), BF16),
        pltpu.VMEM((top, tokens), jnp.int32),
        pltpu.VMEM((tokens, depth), BF16),
        pltpu.VMEM((top, tokens), jnp.int32),
        pltpu.VMEM((tokens, depth), BF16),
        pltpu.VMEM((3, 3, near, CHUNKS, ROWS, lanes), BF16),
        pltpu.VMEM((3, CHUNKS, experts, ROWS, lanes), BF16),
        pltpu.VMEM((2, CHUNKS, experts, ROWS, lanes), BF16),
        pltpu.VMEM((2, CHUNKS, 3, near, ROWS, lanes), BF16),
        pltpu.VMEM((2, tokens, depth), BF16),
        pltpu.VMEM((3, 2, tokens, depth), BF16),
        pltpu.VMEM((2, 2, top, tokens), jnp.int32),
        pltpu.VMEM((full_h, depth), BF16),
        pltpu.VMEM((full_h, depth), BF16),
        pltpu.VMEM((rows, depth), BF16),
        pltpu.VMEM((rows, depth), BF16),
        pltpu.VMEM((rows, depth), BF16),
        pltpu.VMEM((rows, full_h), F32),
        pltpu.VMEM((rows, full_h), F32),
        pltpu.VMEM((rows, full_h), BF16),
        pltpu.VMEM((rows, full_h), BF16),
        pltpu.VMEM((rows, full_h), BF16),
        pltpu.VMEM((max(ROWS, experts * tail), wide), BF16),
        pltpu.VMEM((full_h, depth), BF16),
        pltpu.VMEM((full_h, depth), BF16),
        pltpu.VMEM((6, q if tail else 1, tokens, picked), BF16),
        pltpu.VMEM((q, max(ROWS, near * tail), near * ROWS), BF16),
        pltpu.VMEM((2, tokens, depth), F32),
        pltpu.VMEM((2, 2, tokens, depth), BF16),
        pltpu.VMEM((2, tokens, depth), BF16),
        pltpu.VMEM((2, tokens, depth), BF16),
    ]
    grant = sum(math.prod(b.shape) * jnp.dtype(b.dtype).itemsize for b in buffers) + 3 * 1024 * 1024
    anywhere = pl.BlockSpec(memory_space=pl.ANY)
    dma = pltpu.SemaphoreType.DMA
    states = jax.ShapeDtypeStruct((tokens, depth), BF16)
    parts = jax.ShapeDtypeStruct((sections, own_h, depth), BF16)
    operands = (fwd_states[0], fwd_routes[0].T, bwd_states[0], bwd_routes[0].T, bwd_cot[0], w_in[0], w_out[0])
    next_states, prev_cot, part_in, part_out = pl.pallas_call(
        functools.partial(kernel, experts, sections, main, tail),
        out_shape=(states, states, parts, parts),
        in_specs=[pl.BlockSpec(memory_space=pltpu.HBM)] * 7,
        out_specs=(anywhere,) * 4,
        scratch_shapes=[
            *buffers,
            dma((5,)), dma((3,)), dma((3, 2, CHUNKS)), dma((2,)), dma((2, 2)), dma((3, 3)), dma((3, CHUNKS)),
            dma((2,)), dma((2,)), dma((2, CHUNKS, 3)), dma((2, 2)), dma((2, CHUNKS)),
            dma((2,)), dma((2,)), dma((2,)), dma((2,)), dma((2,)), dma((2,)),
        ],
        compiler_params=pltpu.CompilerParams(
            collective_id=0, has_side_effects=True, vmem_limit_bytes=grant
        ),
    )(*(pltpu.with_memory_space_constraint(v, pltpu.HBM) for v in operands))
    grads = jax.ShapeDtypeStruct((own_h, depth), F32)
    next_states, prev_cot, grad_in, grad_out = pl.pallas_call(
        finish,
        out_shape=(states, states, grads, grads),
        in_specs=[anywhere] * 2 + [pl.BlockSpec(memory_space=pltpu.VMEM)] * 2,
        out_specs=(pl.BlockSpec(memory_space=pltpu.HBM),) * 4,
        scratch_shapes=[pltpu.VMEM((own_h, depth), F32), pltpu.VMEM((own_h, depth), F32), dma((4,))],
        compiler_params=pltpu.CompilerParams(vmem_limit_bytes=own_h * depth * 8 + 2 * 1024 * 1024),
    )(next_states, prev_cot, part_in, part_out)
    return next_states[None], prev_cot[None], grad_in[None], grad_out[None]


def solution(mesh):
    in_specs = (P("section", "expert", None),) * 5 + (P("expert", "section", None),) * 2
    out_specs = (P("section", "expert", None),) * 2 + (P("expert", "section", None),) * 2
    return jax.shard_map(
        per_device, mesh=mesh, in_specs=in_specs, out_specs=out_specs, check_vma=False
    )
```

```python
import functools
import math
import jax
import jax.numpy as jnp
from jax import lax
from jax.experimental import pallas as pl
from jax.experimental.pallas import tpu as pltpu
from jax.sharding import PartitionSpec as P

EPSILON = 1e-06
CHUNKS = 4
ROWS = 16
F32, BF16 = jnp.float32, jnp.bfloat16
NT = (((1,), (1,)), ((), ()))
NN = (((1,), (0,)), ((), ()))
TN = (((0,), (0,)), ((), ()))
FWD, BWD, COT = 0, 1, 2


def mm(a, b, dims):
    return lax.dot_general(a, b, dims, preferred_element_type=F32)


def kernel(
    experts, sections, main, tail,
    xf_hbm, rf_hbm, xb_hbm, rb_hbm, g_hbm, win_hbm, wout_hbm,
    next_ref, prev_ref, gin_ref, gout_ref,
    xf_ref, rf_ref, xb_ref, rb_ref, g_ref,
    send, recv, home, back, u_tok, far_tok, far_routes, w_in, w_out, rows_u, rows_g, rows_f, act, slope, hid, side, front,
    tail_rows, part_in, part_out, table, spread, near_sum, far_send, far_part, carried, result, final,
    loaded, tok_send, tok_recv, route_send, route_recv, near_send, near_recv, home_near, home_far, back_recv,
    cross_send, cross_recv, w_send, w_recv, p_send, p_recv, s_send, s_recv, carry_recv, final_sem,
):
    tokens, depth = xf_hbm.shape
    wide = depth // CHUNKS
    blocks = main // ROWS
    q = ROWS // tail if tail else wide // 256
    thin = wide // q
    own_h = win_hbm.shape[0]
    near = experts // 2
    quarter = experts // 4
    span = near * ROWS
    n_main = experts * main
    me = lax.axis_index("expert")
    sec = lax.axis_index("section")
    half = me // near
    place = lax.rem(me, near)
    column = lax.rem(me, quarter)
    layer = place // quarter
    outward = jnp.where(half == 0, 1 - layer, layer)
    inner = outward == 0
    hub_layer = 1 + half
    my_relay = (2 - half) * quarter + column

    def source(r):
        return (2 - half + r * (1 - 2 * half)) * quarter + column

    def cols(c):
        return pl.ds(pl.multiple_of(c * wide, wide), wide)

    def strip(c, j):
        return pl.ds(pl.multiple_of(c * wide + j * thin, thin), thin)

    loads = [
        pltpu.make_async_copy(src, dst, loaded.at[i])
        for i, (src, dst) in enumerate(
            ((g_hbm, g_ref), (rb_hbm, rb_ref), (rf_hbm, rf_ref), (xb_hbm, xb_ref), (xf_hbm, xf_ref))
        )
    ]
    for load in loads:
        load.start()

    barrier = pltpu.get_barrier_semaphore()

    @pl.loop(1, near)
    def _(k):
        pl.semaphore_signal(barrier, inc=1, device_id={"expert": half * near + lax.rem(place + k, near)})

    @pl.loop(1, sections)
    def _(k):
        pl.semaphore_signal(barrier, inc=1, device_id={"section": lax.rem(sec + k, sections)})

    before, after = lax.rem(sec + sections - 1, sections), lax.rem(sec + 1, sections)
    pl.semaphore_signal(barrier, inc=1, device_id={"expert": my_relay})
    pl.semaphore_signal(barrier, inc=1, device_id={"expert": my_relay, "section": before})

    @pl.when(inner)
    def _():
        pl.semaphore_signal(barrier, inc=1, device_id={"expert": source(1)})

    own_rows = pl.ds(pl.multiple_of(sec * own_h, own_h), own_h)

    def routing(which, routes):
        lane_e = lax.broadcasted_iota(jnp.int32, (tokens, near), 1).astype(F32)
        row = lax.broadcasted_iota(jnp.int32, (tokens, tokens), 0)
        col = lax.broadcasted_iota(jnp.int32, (tokens, tokens), 1)
        names = (routes - half * near).astype(F32).astype(BF16)
        columns = mm((row == col).astype(F32).astype(BF16), names, NT)
        named = [columns[:, k : k + 1] for k in range(routes.shape[0])]
        hits = [(i == lane_e).astype(F32) for i in named]
        counts = functools.reduce(jnp.add, hits)
        rank = mm((row > col).astype(F32).astype(BF16), counts.astype(BF16), NN)
        spots = []
        for i, h in zip(named, hits):
            p = jnp.sum(h * rank, axis=1, keepdims=True)
            slot = jnp.full_like(p, -1.0)
            for b in range(blocks):
                low = b * ROWS
                slot = jnp.where((p >= low) & (p < low + ROWS), b * span + i * ROWS + (p - low), slot)
            spots.append((i, p, slot))
        lanes = table.shape[-1]
        lane = lax.broadcasted_iota(jnp.int32, (tokens, lanes), 1).astype(F32)
        for j in range(table.shape[1]):
            hit = jnp.zeros((tokens, lanes), F32)
            for i, p, slot in spots:
                if tail:
                    slot = jnp.where(p >= main, blocks * span + i * ROWS + j * tail + (p - main), slot)
                slot = jnp.where((i >= 0) & (i < near), slot, -1.0)
                hit = jnp.where(lane == slot, 1.0, hit)
            table[which, j] = hit.astype(BF16)

    def normalize(x_ref, which):
        @pl.loop(0, tokens // 16)
        def _(i):
            rows = pl.ds(pl.multiple_of(i * 16, 16), 16)
            x = x_ref[rows, :].astype(F32)
            inv = lax.rsqrt(jnp.mean(x * x, axis=-1, keepdims=True) + EPSILON)
            u_tok[which, rows, :] = (x * inv).astype(BF16)

    def picks(which, j):
        return table[which, j if tail else 0]

    def dispatch(stream, k, c, src):
        which = min(stream, 1) * 3 + k
        total = None
        for j in range(q):
            out = mm(picks(which, j), src[:, strip(c, j)], TN)
            for b in range(blocks):
                send[stream, k, :, c, :, b * wide + j * thin : b * wide + (j + 1) * thin] = (
                    out[b * span : (b + 1) * span].astype(BF16).reshape(near, ROWS, thin)
                )
            if tail:
                rest = out[blocks * span :]
                total = rest if total is None else total + rest
        if tail:
            send[stream, k, :, c, :, blocks * wide :] = total.astype(BF16).reshape(near, ROWS, thin)

    def to_near(stream, k, c, origin):
        pltpu.make_async_copy(
            send.at[stream, k, place, c], recv.at[stream, c, origin], near_recv.at[stream, c]
        ).start()

        @pl.loop(1, near)
        def _(i):
            spot = lax.rem(place + i, near)
            pltpu.make_async_remote_copy(
                src_ref=send.at[stream, k, spot, c],
                dst_ref=recv.at[stream, c, origin],
                send_sem=near_send.at[stream, k],
                recv_sem=near_recv.at[stream, c],
                device_id={"expert": half * near + spot},
            ).start()

    def own_tokens(stream, src):
        @pl.loop(0, CHUNKS)
        def _(c):
            dispatch(stream, 0, c, src)
            to_near(stream, 0, c, me)

    def to_relay(stream, src):
        @pl.loop(0, CHUNKS)
        def _(c):
            pltpu.make_async_remote_copy(
                src_ref=src.at[:, cols(c)], dst_ref=far_tok.at[stream, outward, :, cols(c)],
                send_sem=tok_send.at[stream], recv_sem=tok_recv.at[stream, outward, c],
                device_id={"expert": my_relay},
            ).start()

    def routes_to_relay(micro, src):
        pltpu.make_async_remote_copy(
            src_ref=src, dst_ref=far_routes.at[micro, outward],
            send_sem=route_send.at[micro], recv_sem=route_recv.at[micro, outward],
            device_id={"expert": my_relay},
        ).start()

    def relay_routes(micro):
        @pl.loop(0, 2)
        def _(r):
            mine = far_routes.at[micro, r]
            pltpu.make_async_copy(mine, mine, route_recv.at[micro, r]).wait()
            routing(micro * 3 + 1 + r, far_routes[micro, r])

    def relay(stream, r, low, high):
        @pl.loop(low, high)
        def _(c):
            block = far_tok.at[stream, r, :, cols(c)]
            pltpu.make_async_copy(block, block, tok_recv.at[stream, r, c]).wait()
            dispatch(stream, 1 + r, c, far_tok.at[stream, r])
            to_near(stream, 1 + r, c, source(r))

    def contract(stream, rows_ref, weight, total, low=0, high=CHUNKS):
        if low == 0:
            total[...] = jnp.zeros_like(total)

        @pl.loop(low, high)
        def _(c):
            buf = recv.at[stream, c]
            pltpu.make_async_copy(buf, buf, near_recv.at[stream, c]).wait()
            for b in range(blocks):
                rows_ref[b * experts * ROWS : (b + 1) * experts * ROWS, cols(c)] = buf[
                    :, :, b * wide : (b + 1) * wide
                ].reshape(experts * ROWS, wide)
            if tail:
                for h in range(2):
                    packed = buf[h * near : (h + 1) * near, :, blocks * wide :].reshape(span, thin)
                    for j in range(q):
                        rows_ref[n_main + h * near * tail : n_main + (h + 1) * near * tail, strip(c, j)] = mm(
                            spread[j], packed, NN
                        ).astype(BF16)
            total[...] += mm(rows_ref[:, cols(c)], weight[:, cols(c)], NT)

    def expand(act_rows, weight, slot):
        @pl.loop(0, CHUNKS)
        def _(c):
            buf = home.at[slot, c]
            step = min(512, wide)
            for i in range(wide // step):
                part = pl.ds(pl.multiple_of(c * wide + i * step, step), step)
                out = mm(act_rows[...], weight[:, part], NN).astype(BF16)
                for b in range(blocks):
                    buf[:, :, b * wide + i * step : b * wide + (i + 1) * step] = out[
                        b * experts * ROWS : (b + 1) * experts * ROWS
                    ].reshape(experts, ROWS, step)
                if tail:
                    tail_rows[:, i * step : (i + 1) * step] = out[n_main:]
            if tail:
                for h in range(2):
                    total = None
                    for j in range(q):
                        block = tail_rows[h * near * tail : (h + 1) * near * tail, j * thin : (j + 1) * thin]
                        moved = mm(spread[j], block, TN)
                        total = moved if total is None else total + moved
                    buf[h * near : (h + 1) * near, :, blocks * wide :] = total.astype(BF16).reshape(
                        near, ROWS, thin
                    )
            give_far(slot, c)

    def give_far(slot, c):
        for r in range(2):
            @pl.loop(0, quarter)
            def _(k):
                col = lax.rem(column + k, quarter)
                hub = hub_layer * quarter + col
                block = home.at[slot, c, (2 - half + r * (1 - 2 * half)) * quarter + col]
                there = back.at[slot, c, 1 + r, place]

                @pl.when(hub == me)
                def _():
                    pltpu.make_async_copy(block, there, back_recv.at[slot, c, 1 + r]).start()

                @pl.when(hub != me)
                def _():
                    pltpu.make_async_remote_copy(
                        src_ref=block, dst_ref=there,
                        send_sem=home_far.at[slot], recv_sem=back_recv.at[slot, c, 1 + r],
                        device_id={"expert": hub},
                    ).start()

    def give_near(slot):
        @pl.loop(0, CHUNKS)
        def _(c):
            pltpu.make_async_copy(
                home.at[slot, c, me], back.at[slot, c, 0, place], back_recv.at[slot, c, 0]
            ).start()

            @pl.loop(1, near)
            def _(k):
                peer = half * near + lax.rem(place + k, near)
                pltpu.make_async_remote_copy(
                    src_ref=home.at[slot, c, peer], dst_ref=back.at[slot, c, 0, place],
                    send_sem=home_near.at[slot], recv_sem=back_recv.at[slot, c, 0],
                    device_id={"expert": peer},
                ).start()

    def combine(slot, c, k, out_ref):
        buf = back.at[slot, c, k]
        pltpu.make_async_copy(buf, buf, back_recv.at[slot, c, k]).wait()
        for j in range(q):
            pieces = [
                buf[:, :, b * wide + j * thin : b * wide + (j + 1) * thin].reshape(span, thin) for b in range(blocks)
            ]
            if tail:
                pieces.append(buf[:, :, blocks * wide :].reshape(span, thin))
            out = mm(picks(slot * 3 + k, j), jnp.concatenate(pieces, axis=0), NN)
            out_ref[:, strip(c, j)] = out.astype(out_ref.dtype)

    def cross(slot, c, r):
        combine(slot, c, 1 + r, far_send.at[slot, r])
        pltpu.make_async_remote_copy(
            src_ref=far_send.at[slot, r, :, cols(c)], dst_ref=far_part.at[slot, :, cols(c)],
            send_sem=cross_send.at[slot, r], recv_sem=cross_recv.at[slot, c],
            device_id={"expert": source(r), "section": after if slot == 0 else sec},
        ).start()

    def cross_range(slot, r, low, high):
        @pl.loop(low, high)
        def _(c):
            cross(slot, c, r)

    def own_sum(slot):
        @pl.loop(0, CHUNKS)
        def _(c):
            combine(slot, c, 0, near_sum.at[slot])

    def crossed(slot, c):
        block = far_part.at[slot, :, cols(c)]
        pltpu.make_async_copy(block, block, cross_recv.at[slot, c]).wait()

    def weight_terms(left, right, part):
        step = min(512, depth)

        @pl.loop(0, depth // step)
        def _(j):
            sl = pl.ds(pl.multiple_of(j * step, step), step)
            part[:, sl] = mm(left[...], right[:, sl], TN).astype(BF16)

    def share(i, part, out):
        pltpu.make_async_copy(part.at[own_rows], out.at[sec], p_recv.at[i]).start()

        @pl.loop(1, sections)
        def _(k):
            peer = lax.rem(sec + k, sections)
            pltpu.make_async_remote_copy(
                src_ref=part.at[pl.ds(pl.multiple_of(peer * own_h, own_h), own_h)],
                dst_ref=out.at[sec],
                send_sem=p_send.at[i], recv_sem=p_recv.at[i],
                device_id={"section": peer},
            ).start()

    outer = jnp.logical_not(inner)
    pl.semaphore_wait(barrier, near + sections - 1 + jnp.where(inner, 3, 0))
    routes_to_relay(1, rb_hbm)
    routes_to_relay(0, rf_hbm)

    @pl.when(outer)
    def _():
        to_relay(COT, g_hbm)

    for load in loads[:4]:
        load.wait()
    normalize(xb_ref, 1)

    @pl.when(outer)
    def _():
        to_relay(BWD, u_tok.at[1])

    @pl.when(inner)
    def _():
        to_relay(COT, g_ref)
        to_relay(BWD, u_tok.at[1])

    routing(3, rb_ref[...])
    own_tokens(COT, g_ref)
    own_tokens(BWD, u_tok.at[1])
    loads[4].wait()
    normalize(xf_ref, 0)
    routing(0, rf_ref[...])

    for i, (src, dst) in enumerate(((win_hbm, w_in), (wout_hbm, w_out))):
        pltpu.make_async_copy(src, dst.at[own_rows], w_recv.at[i]).start()

        @pl.loop(1, sections)
        def _(k):
            pltpu.make_async_remote_copy(
                src_ref=src, dst_ref=dst.at[own_rows],
                send_sem=w_send.at[i], recv_sem=w_recv.at[i],
                device_id={"section": lax.rem(sec + k, sections)},
            ).start()

    if tail:
        shape = (near * tail, span)
        row = lax.broadcasted_iota(jnp.int32, shape, 0).astype(F32)
        col = lax.broadcasted_iota(jnp.int32, shape, 1).astype(F32)
        start = row + jnp.floor((row + 0.5) * (1.0 / tail)) * (ROWS - tail)
        for j in range(q):
            spread[j] = jnp.where(col == start + j * tail, 1.0, 0.0).astype(BF16)

    split = CHUNKS // 2
    last = CHUNKS - 1

    @pl.when(outer)
    def _():
        own_tokens(FWD, u_tok.at[0])

    @pl.when(inner)
    def _():
        to_relay(FWD, u_tok.at[0])
        relay_routes(1)
        relay(COT, 1, 0, CHUNKS)
        relay(BWD, 1, 0, CHUNKS)
        relay_routes(0)
        relay(COT, 0, 0, CHUNKS)
        relay(BWD, 0, 0, split)

    for i, dst in enumerate((w_in, w_out)):
        pltpu.make_async_copy(dst, dst, w_recv.at[i]).wait()

    contract(COT, rows_g, w_out, slope)

    @pl.when(inner)
    def _():
        relay(BWD, 0, split, CHUNKS)
        own_tokens(FWD, u_tok.at[0])

    contract(BWD, rows_u, w_in, act, 0, last)

    @pl.when(outer)
    def _():
        to_relay(FWD, u_tok.at[0])

    contract(BWD, rows_u, w_in, act, last, CHUNKS)
    sigma = jax.nn.sigmoid(act[...])
    hid[...] = (slope[...] * (sigma * (1.0 + act[...] * (1.0 - sigma)))).astype(BF16)
    expand(hid, w_in, 1)
    side[...] = jax.nn.silu(act[...]).astype(BF16)

    @pl.when(inner)
    def _():
        relay(FWD, 1, 0, CHUNKS)
        relay(FWD, 0, 0, last)
        cross_range(1, 0, 0, 1)
        relay(FWD, 0, last, CHUNKS)
        give_near(1)
        cross_range(1, 0, 1, CHUNKS)

    @pl.when(outer)
    def _():
        give_near(1)

    contract(FWD, rows_f, w_in, act)
    front[...] = jax.nn.silu(act[...]).astype(BF16)

    @pl.when(inner)
    def _():
        cross_range(1, 1, 0, split)

    expand(front, w_out, 0)
    give_near(0)

    @pl.when(inner)
    def _():
        cross_range(1, 1, split, CHUNKS)

    weight_terms(hid, rows_u, part_in)
    share(0, part_in, gin_ref)
    weight_terms(side, rows_g, part_out)
    share(1, part_out, gout_ref)
    own_sum(1)

    @pl.when(inner)
    def _():
        @pl.loop(0, CHUNKS)
        def _(c):
            cross(0, c, 1)
            cross(0, c, 0)

    for c in range(CHUNKS):
        crossed(1, c)

    @pl.loop(0, tokens // 16)
    def _(i):
        rows = pl.ds(pl.multiple_of(i * 16, 16), 16)
        x = xb_ref[rows, :].astype(F32)
        total = near_sum[1, rows, :] + far_part[1, rows, :].astype(F32)
        inv = lax.rsqrt(jnp.mean(x * x, axis=-1, keepdims=True) + EPSILON)
        proj = jnp.mean(total * x, axis=-1, keepdims=True)
        grad = g_ref[rows, :].astype(F32) + inv * total - x * (inv * inv * inv) * proj
        result[rows, :] = grad.astype(BF16)

    to_prev = pltpu.make_async_remote_copy(
        src_ref=result, dst_ref=prev_ref, send_sem=s_send.at[1], recv_sem=s_recv.at[0],
        device_id={"section": lax.rem(sec + sections - 1, sections)},
    )
    to_prev.start()

    @pl.loop(0, CHUNKS)
    def _(c):
        combine(0, c, 0, near_sum.at[0])

        @pl.loop(0, tokens // 16)
        def _(i):
            rows = pl.ds(pl.multiple_of(i * 16, 16), 16)
            near_sum[0, rows, cols(c)] += xf_ref[rows, cols(c)].astype(F32)

        pltpu.make_async_remote_copy(
            src_ref=near_sum.at[0, :, cols(c)], dst_ref=carried.at[:, cols(c)],
            send_sem=s_send.at[0], recv_sem=carry_recv.at[c],
            device_id={"section": after},
        ).start()

    for i, (src, out) in enumerate(((win_hbm, gin_ref), (wout_hbm, gout_ref))):
        pltpu.make_async_copy(out, out, p_recv.at[i]).wait()

        @pl.loop(1, sections)
        def _(k):
            pltpu.make_async_copy(src, src, w_send.at[i]).wait()
            pltpu.make_async_copy(src, src, p_send.at[i]).wait()

    def drain(ref, sem):
        pltpu.make_async_copy(ref, ref, sem).wait()

    for stream in range(3):
        drain(g_ref, tok_send.at[stream])
        drain(send.at[0, 0, pl.ds(0, near - 1)], near_send.at[stream, 0])

    for micro, src in enumerate((rf_ref, rb_ref)):
        drain(src, route_send.at[micro])
    for slot in range(2):
        drain(home.at[0, :, pl.ds(0, near - 1)], home_near.at[slot])

    @pl.when(inner)
    def _():
        for stream in range(3):
            for r in range(2):
                drain(send.at[0, 0, pl.ds(0, near - 1)], near_send.at[stream, 1 + r])
        for slot in range(2):
            drain(home.at[0, :, pl.ds(0, near - 2)], home_far.at[slot])

    @pl.when(jnp.logical_not(inner))
    def _():
        for slot in range(2):
            drain(home.at[0, :, pl.ds(0, near)], home_far.at[slot])

    to_prev.wait()

    @pl.loop(0, CHUNKS)
    def _(c):
        moved = carried.at[:, cols(c)]
        drain(moved, carry_recv.at[c])
        crossed(0, c)

        @pl.loop(0, tokens // 16)
        def _(i):
            rows = pl.ds(pl.multiple_of(i * 16, 16), 16)
            total = carried[rows, cols(c)] + far_part[0, rows, cols(c)].astype(F32)
            final[rows, cols(c)] = total.astype(BF16)

        pltpu.make_async_copy(final.at[:, cols(c)], next_ref.at[:, cols(c)], final_sem).start()

    drain(next_ref, final_sem)

    drain(carried, s_send.at[0])

    @pl.when(inner)
    def _():
        for slot in range(2):
            for r in range(2):
                drain(far_send.at[slot, r], cross_send.at[slot, r])


def finish(next_ref, prev_ref, pin_ref, pout_ref, next_out, prev_out, gin_out, gout_out, sum_in, sum_out, sems):
    own_h = sum_in.shape[0]
    step = own_h // 4
    moves = [
        pltpu.make_async_copy(next_ref, next_out, sems.at[0]),
        pltpu.make_async_copy(prev_ref, prev_out, sems.at[1]),
    ]
    for move in moves:
        move.start()
    for i, (part, total, out) in enumerate(((pin_ref, sum_in, gin_out), (pout_ref, sum_out, gout_out))):
        @pl.loop(0, own_h // step)
        def _(b):
            @pl.loop(0, step // 16)
            def _(j):
                rows = pl.ds(pl.multiple_of(b * step + j * 16, 16), 16)
                total[rows, :] = functools.reduce(
                    jnp.add, [part[k, rows, :].astype(F32) for k in range(part.shape[0])]
                )

            block = pl.ds(pl.multiple_of(b * step, step), step)
            pltpu.make_async_copy(total.at[block], out.at[block], sems.at[2 + i]).start()

    for move in moves:
        move.wait()
    for i, (total, out) in enumerate(((sum_in, gin_out), (sum_out, gout_out))):
        pltpu.make_async_copy(total, out, sems.at[2 + i]).wait()


def per_device(fwd_states, fwd_routes, bwd_states, bwd_routes, bwd_cot, w_in, w_out):
    experts, sections = lax.axis_size("expert"), lax.axis_size("section")
    _, tokens, depth = fwd_states.shape
    top = fwd_routes.shape[2]
    own_h = w_in.shape[1]
    full_h = own_h * sections
    cap = max(2, (5 * tokens * top + 4 * experts - 1) // (4 * experts))
    main, tail = cap // ROWS * ROWS, cap % ROWS
    tail = next(t for t in (0, 2, 4, 8, 16) if t >= tail)
    main, tail = main + tail // ROWS * ROWS, tail % ROWS
    rows = experts * (main + tail)
    near = experts // 2
    wide = depth // CHUNKS
    q = ROWS // tail if tail else wide // 256
    thin = wide // q
    blocks = main // ROWS
    lanes = blocks * wide + (thin if tail else 0)
    picked = (blocks + (1 if tail else 0)) * near * ROWS
    buffers = [
        pltpu.VMEM((tokens, depth), BF16),
        pltpu.VMEM((top, tokens), jnp.int32),
        pltpu.VMEM((tokens, depth), BF16),
        pltpu.VMEM((top, tokens), jnp.int32),
        pltpu.VMEM((tokens, depth), BF16),
        pltpu.VMEM((3, 3, near, CHUNKS, ROWS, lanes), BF16),
        pltpu.VMEM((3, CHUNKS, experts, ROWS, lanes), BF16),
        pltpu.VMEM((2, CHUNKS, experts, ROWS, lanes), BF16),
        pltpu.VMEM((2, CHUNKS, 3, near, ROWS, lanes), BF16),
        pltpu.VMEM((2, tokens, depth), BF16),
        pltpu.VMEM((3, 2, tokens, depth), BF16),
        pltpu.VMEM((2, 2, top, tokens), jnp.int32),
        pltpu.VMEM((full_h, depth), BF16),
        pltpu.VMEM((full_h, depth), BF16),
        pltpu.VMEM((rows, depth), BF16),
        pltpu.VMEM((rows, depth), BF16),
        pltpu.VMEM((rows, depth), BF16),
        pltpu.VMEM((rows, full_h), F32),
        pltpu.VMEM((rows, full_h), F32),
        pltpu.VMEM((rows, full_h), BF16),
        pltpu.VMEM((rows, full_h), BF16),
        pltpu.VMEM((rows, full_h), BF16),
        pltpu.VMEM((max(ROWS, experts * tail), wide), BF16),
        pltpu.VMEM((full_h, depth), BF16),
        pltpu.VMEM((full_h, depth), BF16),
        pltpu.VMEM((6, q if tail else 1, tokens, picked), BF16),
        pltpu.VMEM((q, max(ROWS, near * tail), near * ROWS), BF16),
        pltpu.VMEM((2, tokens, depth), F32),
        pltpu.VMEM((2, 2, tokens, depth), BF16),
        pltpu.VMEM((2, tokens, depth), BF16),
        pltpu.VMEM((tokens, depth), F32),
        pltpu.VMEM((tokens, depth), BF16),
        pltpu.VMEM((tokens, depth), BF16),
    ]
    grant = sum(math.prod(b.shape) * jnp.dtype(b.dtype).itemsize for b in buffers) + 3 * 1024 * 1024
    anywhere = pl.BlockSpec(memory_space=pl.ANY)
    dma = pltpu.SemaphoreType.DMA
    states = jax.ShapeDtypeStruct((tokens, depth), BF16)
    parts = jax.ShapeDtypeStruct((sections, own_h, depth), BF16)
    grads = jax.ShapeDtypeStruct((own_h, depth), F32)
    operands = (fwd_states[0], fwd_routes[0].T, bwd_states[0], bwd_routes[0].T, bwd_cot[0], w_in[0], w_out[0])
    results = pl.pallas_call(
        functools.partial(kernel, experts, sections, main, tail),
        out_shape=(states, states, parts, parts),
        in_specs=[pl.BlockSpec(memory_space=pltpu.HBM)] * 7,
        out_specs=(anywhere,) * 4,
        scratch_shapes=[
            *buffers,
            dma((5,)), dma((3,)), dma((3, 2, CHUNKS)), dma((2,)), dma((2, 2)), dma((3, 3)), dma((3, CHUNKS)),
            dma((2,)), dma((2,)), dma((2, CHUNKS, 3)), dma((2, 2)), dma((2, CHUNKS)),
            dma((2,)), dma((2,)), dma((2,)), dma((2,)), dma((2,)), dma((1,)), dma((CHUNKS,)), dma,
        ],
        compiler_params=pltpu.CompilerParams(
            collective_id=0, has_side_effects=True, vmem_limit_bytes=grant
        ),
    )(*(pltpu.with_memory_space_constraint(v, pltpu.HBM) for v in operands))
    outs = pl.pallas_call(
        finish,
        out_shape=(states, states, grads, grads),
        in_specs=[anywhere] * 2 + [pl.BlockSpec(memory_space=pltpu.VMEM)] * 2,
        out_specs=(pl.BlockSpec(memory_space=pltpu.HBM),) * 4,
        scratch_shapes=[pltpu.VMEM((own_h, depth), F32), pltpu.VMEM((own_h, depth), F32), dma((4,))],
        compiler_params=pltpu.CompilerParams(vmem_limit_bytes=own_h * depth * 8 + 2 * 1024 * 1024),
    )(*results)
    return tuple(out[None] for out in outs)


def solution(mesh):
    in_specs = (P("section", "expert", None),) * 5 + (P("expert", "section", None),) * 2
    out_specs = (P("section", "expert", None),) * 2 + (P("expert", "section", None),) * 2
    return jax.shard_map(
        per_device, mesh=mesh, in_specs=in_specs, out_specs=out_specs, check_vma=False
    )
```

```python
import functools
import math
import jax
import jax.numpy as jnp
from jax import lax
from jax.experimental import pallas as pl
from jax.experimental.pallas import tpu as pltpu
from jax.sharding import PartitionSpec as P

EPSILON = 1e-06
CHUNKS = 4
ROWS = 16
F32, BF16 = jnp.float32, jnp.bfloat16
NT = (((1,), (1,)), ((), ()))
NN = (((1,), (0,)), ((), ()))
TN = (((0,), (0,)), ((), ()))
FWD, BWD, COT = 0, 1, 2


def mm(a, b, dims):
    return lax.dot_general(a, b, dims, preferred_element_type=F32)


def kernel(
    experts, sections, main, tail,
    xf_hbm, rf_hbm, xb_hbm, rb_hbm, g_hbm, win_hbm, wout_hbm,
    next_ref, prev_ref, gin_ref, gout_ref,
    xf_ref, rf_ref, xb_ref, rb_ref, g_ref,
    send, recv, home, back, u_tok, far_tok, far_routes, w_in, w_out, rows_u, rows_g, rows_f, act, slope, hid, side, front,
    tail_rows, part_in, part_out, table, spread, near_sum, far_send, far_part, carried, result, final,
    loaded, tok_send, tok_recv, route_send, route_recv, near_send, near_recv, home_near, home_far, back_recv,
    cross_send, cross_recv, w_send, w_recv, p_send, p_recv, s_send, s_recv, carry_recv, final_sem, go,
):
    tokens, depth = xf_hbm.shape
    wide = depth // CHUNKS
    blocks = main // ROWS
    q = ROWS // tail if tail else wide // 256
    thin = wide // q
    own_h = win_hbm.shape[0]
    near = experts // 2
    quarter = experts // 4
    span = near * ROWS
    n_main = experts * main
    me = lax.axis_index("expert")
    sec = lax.axis_index("section")
    half = me // near
    place = lax.rem(me, near)
    column = lax.rem(me, quarter)
    layer = place // quarter
    outward = jnp.where(half == 0, 1 - layer, layer)
    inner = outward == 0
    hub_layer = 1 + half
    my_relay = (2 - half) * quarter + column

    def source(r):
        return (2 - half + r * (1 - 2 * half)) * quarter + column

    def cols(c):
        return pl.ds(pl.multiple_of(c * wide, wide), wide)

    def strip(c, j):
        return pl.ds(pl.multiple_of(c * wide + j * thin, thin), thin)

    loads = [
        pltpu.make_async_copy(src, dst, loaded.at[i])
        for i, (src, dst) in enumerate(
            ((g_hbm, g_ref), (rb_hbm, rb_ref), (rf_hbm, rf_ref), (xb_hbm, xb_ref), (xf_hbm, xf_ref))
        )
    ]
    for load in loads:
        load.start()

    barrier = pltpu.get_barrier_semaphore()

    before, after = lax.rem(sec + sections - 1, sections), lax.rem(sec + 1, sections)
    host = (me == experts - 1) & (sec == 0)
    guest = jnp.logical_not(host)

    @pl.when(inner)
    def _():
        for r in range(2):
            pl.semaphore_signal(barrier, inc=1, device_id={"expert": source(r)})

    @pl.when(guest)
    def _():
        pl.semaphore_signal(barrier, inc=1, device_id={"expert": experts - 1, "section": 0})

    own_rows = pl.ds(pl.multiple_of(sec * own_h, own_h), own_h)

    def routing(which, routes):
        lane_e = lax.broadcasted_iota(jnp.int32, (tokens, near), 1).astype(F32)
        row = lax.broadcasted_iota(jnp.int32, (tokens, tokens), 0)
        col = lax.broadcasted_iota(jnp.int32, (tokens, tokens), 1)
        names = (routes - half * near).astype(F32).astype(BF16)
        columns = mm((row == col).astype(F32).astype(BF16), names, NT)
        named = [columns[:, k : k + 1] for k in range(routes.shape[0])]
        hits = [(i == lane_e).astype(F32) for i in named]
        counts = functools.reduce(jnp.add, hits)
        rank = mm((row > col).astype(F32).astype(BF16), counts.astype(BF16), NN)
        spots = []
        for i, h in zip(named, hits):
            p = jnp.sum(h * rank, axis=1, keepdims=True)
            slot = jnp.full_like(p, -1.0)
            for b in range(blocks):
                low = b * ROWS
                slot = jnp.where((p >= low) & (p < low + ROWS), b * span + i * ROWS + (p - low), slot)
            spots.append((i, p, slot))
        lanes = table.shape[-1]
        lane = lax.broadcasted_iota(jnp.int32, (tokens, lanes), 1).astype(F32)
        for j in range(table.shape[1]):
            hit = jnp.zeros((tokens, lanes), F32)
            for i, p, slot in spots:
                if tail:
                    slot = jnp.where(p >= main, blocks * span + i * ROWS + j * tail + (p - main), slot)
                slot = jnp.where((i >= 0) & (i < near), slot, -1.0)
                hit = jnp.where(lane == slot, 1.0, hit)
            table[which, j] = hit.astype(BF16)

    def normalize(x_ref, which):
        @pl.loop(0, tokens // 16)
        def _(i):
            rows = pl.ds(pl.multiple_of(i * 16, 16), 16)
            x = x_ref[rows, :].astype(F32)
            inv = lax.rsqrt(jnp.mean(x * x, axis=-1, keepdims=True) + EPSILON)
            u_tok[which, rows, :] = (x * inv).astype(BF16)

    def picks(which, j):
        return table[which, j if tail else 0]

    def dispatch(stream, k, c, src):
        which = min(stream, 1) * 3 + k
        total = None
        for j in range(q):
            out = mm(picks(which, j), src[:, strip(c, j)], TN)
            for b in range(blocks):
                send[stream, k, :, c, :, b * wide + j * thin : b * wide + (j + 1) * thin] = (
                    out[b * span : (b + 1) * span].astype(BF16).reshape(near, ROWS, thin)
                )
            if tail:
                rest = out[blocks * span :]
                total = rest if total is None else total + rest
        if tail:
            send[stream, k, :, c, :, blocks * wide :] = total.astype(BF16).reshape(near, ROWS, thin)

    def to_near(stream, k, c, origin):
        pltpu.make_async_copy(
            send.at[stream, k, place, c], recv.at[stream, c, origin], near_recv.at[stream, c]
        ).start()

        @pl.loop(1, near)
        def _(i):
            spot = lax.rem(place + i, near)
            pltpu.make_async_remote_copy(
                src_ref=send.at[stream, k, spot, c],
                dst_ref=recv.at[stream, c, origin],
                send_sem=near_send.at[stream, k],
                recv_sem=near_recv.at[stream, c],
                device_id={"expert": half * near + spot},
            ).start()

    def own_tokens(stream, src):
        @pl.loop(0, CHUNKS)
        def _(c):
            dispatch(stream, 0, c, src)
            to_near(stream, 0, c, me)

    def to_relay(stream, src):
        @pl.loop(0, CHUNKS)
        def _(c):
            pltpu.make_async_remote_copy(
                src_ref=src.at[:, cols(c)], dst_ref=far_tok.at[stream, outward, :, cols(c)],
                send_sem=tok_send.at[stream], recv_sem=tok_recv.at[stream, outward, c],
                device_id={"expert": my_relay},
            ).start()

    def routes_to_relay(micro, src):
        pltpu.make_async_remote_copy(
            src_ref=src, dst_ref=far_routes.at[micro, outward],
            send_sem=route_send.at[micro], recv_sem=route_recv.at[micro, outward],
            device_id={"expert": my_relay},
        ).start()

    def relay_routes(micro):
        @pl.loop(0, 2)
        def _(r):
            mine = far_routes.at[micro, r]
            pltpu.make_async_copy(mine, mine, route_recv.at[micro, r]).wait()
            routing(micro * 3 + 1 + r, far_routes[micro, r])

    def relay(stream, r, low, high):
        @pl.loop(low, high)
        def _(c):
            block = far_tok.at[stream, r, :, cols(c)]
            pltpu.make_async_copy(block, block, tok_recv.at[stream, r, c]).wait()
            dispatch(stream, 1 + r, c, far_tok.at[stream, r])
            to_near(stream, 1 + r, c, source(r))

    def contract(stream, rows_ref, weight, total, low=0, high=CHUNKS):
        if low == 0:
            total[...] = jnp.zeros_like(total)

        @pl.loop(low, high)
        def _(c):
            buf = recv.at[stream, c]
            pltpu.make_async_copy(buf, buf, near_recv.at[stream, c]).wait()
            for b in range(blocks):
                rows_ref[b * experts * ROWS : (b + 1) * experts * ROWS, cols(c)] = buf[
                    :, :, b * wide : (b + 1) * wide
                ].reshape(experts * ROWS, wide)
            if tail:
                for h in range(2):
                    packed = buf[h * near : (h + 1) * near, :, blocks * wide :].reshape(span, thin)
                    for j in range(q):
                        rows_ref[n_main + h * near * tail : n_main + (h + 1) * near * tail, strip(c, j)] = mm(
                            spread[j], packed, NN
                        ).astype(BF16)
            total[...] += mm(rows_ref[:, cols(c)], weight[:, cols(c)], NT)

    def expand(act_rows, weight, slot):
        @pl.loop(0, CHUNKS)
        def _(c):
            buf = home.at[slot, c]
            step = min(512, wide)
            for i in range(wide // step):
                part = pl.ds(pl.multiple_of(c * wide + i * step, step), step)
                out = mm(act_rows[...], weight[:, part], NN).astype(BF16)
                for b in range(blocks):
                    buf[:, :, b * wide + i * step : b * wide + (i + 1) * step] = out[
                        b * experts * ROWS : (b + 1) * experts * ROWS
                    ].reshape(experts, ROWS, step)
                if tail:
                    tail_rows[:, i * step : (i + 1) * step] = out[n_main:]
            if tail:
                for h in range(2):
                    total = None
                    for j in range(q):
                        block = tail_rows[h * near * tail : (h + 1) * near * tail, j * thin : (j + 1) * thin]
                        moved = mm(spread[j], block, TN)
                        total = moved if total is None else total + moved
                    buf[h * near : (h + 1) * near, :, blocks * wide :] = total.astype(BF16).reshape(
                        near, ROWS, thin
                    )
            give_far(slot, c)

    def give_far(slot, c):
        for r in range(2):
            @pl.loop(0, quarter)
            def _(k):
                col = lax.rem(column + k, quarter)
                hub = hub_layer * quarter + col
                block = home.at[slot, c, (2 - half + r * (1 - 2 * half)) * quarter + col]
                there = back.at[slot, c, 1 + r, place]

                @pl.when(hub == me)
                def _():
                    pltpu.make_async_copy(block, there, back_recv.at[slot, c, 1 + r]).start()

                @pl.when(hub != me)
                def _():
                    pltpu.make_async_remote_copy(
                        src_ref=block, dst_ref=there,
                        send_sem=home_far.at[slot], recv_sem=back_recv.at[slot, c, 1 + r],
                        device_id={"expert": hub},
                    ).start()

    def give_near(slot):
        @pl.loop(0, CHUNKS)
        def _(c):
            pltpu.make_async_copy(
                home.at[slot, c, me], back.at[slot, c, 0, place], back_recv.at[slot, c, 0]
            ).start()

            @pl.loop(1, near)
            def _(k):
                peer = half * near + lax.rem(place + k, near)
                pltpu.make_async_remote_copy(
                    src_ref=home.at[slot, c, peer], dst_ref=back.at[slot, c, 0, place],
                    send_sem=home_near.at[slot], recv_sem=back_recv.at[slot, c, 0],
                    device_id={"expert": peer},
                ).start()

    def combine(slot, c, k, out_ref):
        buf = back.at[slot, c, k]
        pltpu.make_async_copy(buf, buf, back_recv.at[slot, c, k]).wait()
        for j in range(q):
            pieces = [
                buf[:, :, b * wide + j * thin : b * wide + (j + 1) * thin].reshape(span, thin) for b in range(blocks)
            ]
            if tail:
                pieces.append(buf[:, :, blocks * wide :].reshape(span, thin))
            out = mm(picks(slot * 3 + k, j), jnp.concatenate(pieces, axis=0), NN)
            out_ref[:, strip(c, j)] = out.astype(out_ref.dtype)

    def cross(slot, c, r):
        combine(slot, c, 1 + r, far_send.at[slot, r])
        pltpu.make_async_remote_copy(
            src_ref=far_send.at[slot, r, :, cols(c)], dst_ref=far_part.at[slot, :, cols(c)],
            send_sem=cross_send.at[slot, r], recv_sem=cross_recv.at[slot, c],
            device_id={"expert": source(r), "section": after if slot == 0 else sec},
        ).start()

    def cross_range(slot, r, low, high):
        @pl.loop(low, high)
        def _(c):
            cross(slot, c, r)

    def own_sum(slot):
        @pl.loop(0, CHUNKS)
        def _(c):
            combine(slot, c, 0, near_sum.at[slot])

    def crossed(slot, c):
        block = far_part.at[slot, :, cols(c)]
        pltpu.make_async_copy(block, block, cross_recv.at[slot, c]).wait()

    def weight_terms(left, right, part):
        step = min(512, depth)

        @pl.loop(0, depth // step)
        def _(j):
            sl = pl.ds(pl.multiple_of(j * step, step), step)
            part[:, sl] = mm(left[...], right[:, sl], TN).astype(BF16)

    def share(i, part, out):
        pltpu.make_async_copy(part.at[own_rows], out.at[sec], p_recv.at[i]).start()

        @pl.loop(1, sections)
        def _(k):
            peer = lax.rem(sec + k, sections)
            pltpu.make_async_remote_copy(
                src_ref=part.at[pl.ds(pl.multiple_of(peer * own_h, own_h), own_h)],
                dst_ref=out.at[sec],
                send_sem=p_send.at[i], recv_sem=p_recv.at[i],
                device_id={"section": peer},
            ).start()

    outer = jnp.logical_not(inner)
    pl.semaphore_wait(barrier, 1 + jnp.where(host, experts * sections - 1, 0))

    @pl.when(host)
    def _():
        @pl.loop(0, experts)
        def _(e):
            @pl.loop(0, sections)
            def _(t):
                @pl.when((e != me) | (t != sec))
                def _():
                    pl.semaphore_signal(go, inc=1, device_id={"expert": e, "section": t})

    routes_to_relay(1, rb_hbm)
    routes_to_relay(0, rf_hbm)

    @pl.when(outer)
    def _():
        to_relay(COT, g_hbm)

    for load in loads[:4]:
        load.wait()
    normalize(xb_ref, 1)

    @pl.when(outer)
    def _():
        to_relay(BWD, u_tok.at[1])

    @pl.when(inner)
    def _():
        to_relay(COT, g_ref)
        to_relay(BWD, u_tok.at[1])

    routing(3, rb_ref[...])

    @pl.when(guest)
    def _():
        pl.semaphore_wait(go, 1)

    own_tokens(COT, g_ref)
    own_tokens(BWD, u_tok.at[1])
    loads[4].wait()
    normalize(xf_ref, 0)
    routing(0, rf_ref[...])

    for i, (src, dst) in enumerate(((win_hbm, w_in), (wout_hbm, w_out))):
        pltpu.make_async_copy(src, dst.at[own_rows], w_recv.at[i]).start()

        @pl.loop(1, sections)
        def _(k):
            pltpu.make_async_remote_copy(
                src_ref=src, dst_ref=dst.at[own_rows],
                send_sem=w_send.at[i], recv_sem=w_recv.at[i],
                device_id={"section": lax.rem(sec + k, sections)},
            ).start()

    if tail:
        shape = (near * tail, span)
        row = lax.broadcasted_iota(jnp.int32, shape, 0).astype(F32)
        col = lax.broadcasted_iota(jnp.int32, shape, 1).astype(F32)
        start = row + jnp.floor((row + 0.5) * (1.0 / tail)) * (ROWS - tail)
        for j in range(q):
            spread[j] = jnp.where(col == start + j * tail, 1.0, 0.0).astype(BF16)

    split = CHUNKS // 2
    last = CHUNKS - 1

    @pl.when(outer)
    def _():
        own_tokens(FWD, u_tok.at[0])

    @pl.when(inner)
    def _():
        to_relay(FWD, u_tok.at[0])
        relay_routes(1)
        relay(COT, 1, 0, CHUNKS)
        relay(BWD, 1, 0, CHUNKS)
        relay_routes(0)
        relay(COT, 0, 0, CHUNKS)
        relay(BWD, 0, 0, split)

    for i, dst in enumerate((w_in, w_out)):
        pltpu.make_async_copy(dst, dst, w_recv.at[i]).wait()

    contract(COT, rows_g, w_out, slope)

    @pl.when(inner)
    def _():
        relay(BWD, 0, split, CHUNKS)
        own_tokens(FWD, u_tok.at[0])

    contract(BWD, rows_u, w_in, act, 0, last)

    @pl.when(outer)
    def _():
        to_relay(FWD, u_tok.at[0])

    contract(BWD, rows_u, w_in, act, last, CHUNKS)
    sigma = jax.nn.sigmoid(act[...])
    hid[...] = (slope[...] * (sigma * (1.0 + act[...] * (1.0 - sigma)))).astype(BF16)
    expand(hid, w_in, 1)
    side[...] = jax.nn.silu(act[...]).astype(BF16)

    @pl.when(inner)
    def _():
        relay(FWD, 1, 0, CHUNKS)
        relay(FWD, 0, 0, last)
        cross_range(1, 0, 0, 1)
        relay(FWD, 0, last, CHUNKS)
        give_near(1)
        cross_range(1, 0, 1, CHUNKS)

    @pl.when(outer)
    def _():
        give_near(1)

    contract(FWD, rows_f, w_in, act)
    front[...] = jax.nn.silu(act[...]).astype(BF16)

    @pl.when(inner)
    def _():
        cross_range(1, 1, 0, split)

    expand(front, w_out, 0)
    give_near(0)

    @pl.when(inner)
    def _():
        cross_range(1, 1, split, CHUNKS)

    weight_terms(hid, rows_u, part_in)
    share(0, part_in, gin_ref)
    weight_terms(side, rows_g, part_out)
    share(1, part_out, gout_ref)
    own_sum(1)

    @pl.when(inner)
    def _():
        @pl.loop(0, CHUNKS)
        def _(c):
            cross(0, c, 1)
            cross(0, c, 0)

    for c in range(CHUNKS):
        crossed(1, c)

    @pl.loop(0, tokens // 16)
    def _(i):
        rows = pl.ds(pl.multiple_of(i * 16, 16), 16)
        x = xb_ref[rows, :].astype(F32)
        total = near_sum[1, rows, :] + far_part[1, rows, :].astype(F32)
        inv = lax.rsqrt(jnp.mean(x * x, axis=-1, keepdims=True) + EPSILON)
        proj = jnp.mean(total * x, axis=-1, keepdims=True)
        grad = g_ref[rows, :].astype(F32) + inv * total - x * (inv * inv * inv) * proj
        result[rows, :] = grad.astype(BF16)

    to_prev = pltpu.make_async_remote_copy(
        src_ref=result, dst_ref=prev_ref, send_sem=s_send.at[1], recv_sem=s_recv.at[0],
        device_id={"section": lax.rem(sec + sections - 1, sections)},
    )
    to_prev.start()

    @pl.loop(0, CHUNKS)
    def _(c):
        combine(0, c, 0, near_sum.at[0])

        @pl.loop(0, tokens // 16)
        def _(i):
            rows = pl.ds(pl.multiple_of(i * 16, 16), 16)
            near_sum[0, rows, cols(c)] += xf_ref[rows, cols(c)].astype(F32)

        pltpu.make_async_remote_copy(
            src_ref=near_sum.at[0, :, cols(c)], dst_ref=carried.at[:, cols(c)],
            send_sem=s_send.at[0], recv_sem=carry_recv.at[c],
            device_id={"section": after},
        ).start()

    for i, (src, out) in enumerate(((win_hbm, gin_ref), (wout_hbm, gout_ref))):
        pltpu.make_async_copy(out, out, p_recv.at[i]).wait()

        @pl.loop(1, sections)
        def _(k):
            pltpu.make_async_copy(src, src, w_send.at[i]).wait()
            pltpu.make_async_copy(src, src, p_send.at[i]).wait()

    def drain(ref, sem):
        pltpu.make_async_copy(ref, ref, sem).wait()

    for stream in range(3):
        drain(g_ref, tok_send.at[stream])
        drain(send.at[0, 0, pl.ds(0, near - 1)], near_send.at[stream, 0])

    for micro, src in enumerate((rf_ref, rb_ref)):
        drain(src, route_send.at[micro])
    for slot in range(2):
        drain(home.at[0, :, pl.ds(0, near - 1)], home_near.at[slot])

    @pl.when(inner)
    def _():
        for stream in range(3):
            for r in range(2):
                drain(send.at[0, 0, pl.ds(0, near - 1)], near_send.at[stream, 1 + r])
        for slot in range(2):
            drain(home.at[0, :, pl.ds(0, near - 2)], home_far.at[slot])

    @pl.when(jnp.logical_not(inner))
    def _():
        for slot in range(2):
            drain(home.at[0, :, pl.ds(0, near)], home_far.at[slot])

    to_prev.wait()

    @pl.loop(0, CHUNKS)
    def _(c):
        moved = carried.at[:, cols(c)]
        drain(moved, carry_recv.at[c])
        crossed(0, c)

        @pl.loop(0, tokens // 16)
        def _(i):
            rows = pl.ds(pl.multiple_of(i * 16, 16), 16)
            total = carried[rows, cols(c)] + far_part[0, rows, cols(c)].astype(F32)
            final[rows, cols(c)] = total.astype(BF16)

        pltpu.make_async_copy(final.at[:, cols(c)], next_ref.at[:, cols(c)], final_sem).start()

    drain(next_ref, final_sem)

    drain(carried, s_send.at[0])

    @pl.when(inner)
    def _():
        for slot in range(2):
            for r in range(2):
                drain(far_send.at[slot, r], cross_send.at[slot, r])


def finish(next_ref, prev_ref, pin_ref, pout_ref, next_out, prev_out, gin_out, gout_out, sum_in, sum_out, sems):
    own_h = sum_in.shape[0]
    step = own_h // 4
    moves = [
        pltpu.make_async_copy(next_ref, next_out, sems.at[0]),
        pltpu.make_async_copy(prev_ref, prev_out, sems.at[1]),
    ]
    for move in moves:
        move.start()
    for i, (part, total, out) in enumerate(((pin_ref, sum_in, gin_out), (pout_ref, sum_out, gout_out))):
        @pl.loop(0, own_h // step)
        def _(b):
            @pl.loop(0, step // 16)
            def _(j):
                rows = pl.ds(pl.multiple_of(b * step + j * 16, 16), 16)
                total[rows, :] = functools.reduce(
                    jnp.add, [part[k, rows, :].astype(F32) for k in range(part.shape[0])]
                )

            block = pl.ds(pl.multiple_of(b * step, step), step)
            pltpu.make_async_copy(total.at[block], out.at[block], sems.at[2 + i]).start()

    for move in moves:
        move.wait()
    for i, (total, out) in enumerate(((sum_in, gin_out), (sum_out, gout_out))):
        pltpu.make_async_copy(total, out, sems.at[2 + i]).wait()


def per_device(fwd_states, fwd_routes, bwd_states, bwd_routes, bwd_cot, w_in, w_out):
    experts, sections = lax.axis_size("expert"), lax.axis_size("section")
    _, tokens, depth = fwd_states.shape
    top = fwd_routes.shape[2]
    own_h = w_in.shape[1]
    full_h = own_h * sections
    cap = max(2, (5 * tokens * top + 4 * experts - 1) // (4 * experts))
    main, tail = cap // ROWS * ROWS, cap % ROWS
    tail = next(t for t in (0, 2, 4, 8, 16) if t >= tail)
    main, tail = main + tail // ROWS * ROWS, tail % ROWS
    rows = experts * (main + tail)
    near = experts // 2
    wide = depth // CHUNKS
    q = ROWS // tail if tail else wide // 256
    thin = wide // q
    blocks = main // ROWS
    lanes = blocks * wide + (thin if tail else 0)
    picked = (blocks + (1 if tail else 0)) * near * ROWS
    buffers = [
        pltpu.VMEM((tokens, depth), BF16),
        pltpu.VMEM((top, tokens), jnp.int32),
        pltpu.VMEM((tokens, depth), BF16),
        pltpu.VMEM((top, tokens), jnp.int32),
        pltpu.VMEM((tokens, depth), BF16),
        pltpu.VMEM((3, 3, near, CHUNKS, ROWS, lanes), BF16),
        pltpu.VMEM((3, CHUNKS, experts, ROWS, lanes), BF16),
        pltpu.VMEM((2, CHUNKS, experts, ROWS, lanes), BF16),
        pltpu.VMEM((2, CHUNKS, 3, near, ROWS, lanes), BF16),
        pltpu.VMEM((2, tokens, depth), BF16),
        pltpu.VMEM((3, 2, tokens, depth), BF16),
        pltpu.VMEM((2, 2, top, tokens), jnp.int32),
        pltpu.VMEM((full_h, depth), BF16),
        pltpu.VMEM((full_h, depth), BF16),
        pltpu.VMEM((rows, depth), BF16),
        pltpu.VMEM((rows, depth), BF16),
        pltpu.VMEM((rows, depth), BF16),
        pltpu.VMEM((rows, full_h), F32),
        pltpu.VMEM((rows, full_h), F32),
        pltpu.VMEM((rows, full_h), BF16),
        pltpu.VMEM((rows, full_h), BF16),
        pltpu.VMEM((rows, full_h), BF16),
        pltpu.VMEM((max(ROWS, experts * tail), wide), BF16),
        pltpu.VMEM((full_h, depth), BF16),
        pltpu.VMEM((full_h, depth), BF16),
        pltpu.VMEM((6, q if tail else 1, tokens, picked), BF16),
        pltpu.VMEM((q, max(ROWS, near * tail), near * ROWS), BF16),
        pltpu.VMEM((2, tokens, depth), F32),
        pltpu.VMEM((2, 2, tokens, depth), BF16),
        pltpu.VMEM((2, tokens, depth), BF16),
        pltpu.VMEM((tokens, depth), F32),
        pltpu.VMEM((tokens, depth), BF16),
        pltpu.VMEM((tokens, depth), BF16),
    ]
    grant = sum(math.prod(b.shape) * jnp.dtype(b.dtype).itemsize for b in buffers) + 3 * 1024 * 1024
    anywhere = pl.BlockSpec(memory_space=pl.ANY)
    dma = pltpu.SemaphoreType.DMA
    states = jax.ShapeDtypeStruct((tokens, depth), BF16)
    parts = jax.ShapeDtypeStruct((sections, own_h, depth), BF16)
    grads = jax.ShapeDtypeStruct((own_h, depth), F32)
    operands = (fwd_states[0], fwd_routes[0].T, bwd_states[0], bwd_routes[0].T, bwd_cot[0], w_in[0], w_out[0])
    results = pl.pallas_call(
        functools.partial(kernel, experts, sections, main, tail),
        out_shape=(states, states, parts, parts),
        in_specs=[pl.BlockSpec(memory_space=pltpu.HBM)] * 7,
        out_specs=(anywhere,) * 4,
        scratch_shapes=[
            *buffers,
            dma((5,)), dma((3,)), dma((3, 2, CHUNKS)), dma((2,)), dma((2, 2)), dma((3, 3)), dma((3, CHUNKS)),
            dma((2,)), dma((2,)), dma((2, CHUNKS, 3)), dma((2, 2)), dma((2, CHUNKS)),
            dma((2,)), dma((2,)), dma((2,)), dma((2,)), dma((2,)), dma((1,)), dma((CHUNKS,)), dma, pltpu.SemaphoreType.REGULAR,
        ],
        compiler_params=pltpu.CompilerParams(
            collective_id=0, has_side_effects=True, vmem_limit_bytes=grant
        ),
    )(*(pltpu.with_memory_space_constraint(v, pltpu.HBM) for v in operands))
    outs = pl.pallas_call(
        finish,
        out_shape=(states, states, grads, grads),
        in_specs=[anywhere] * 2 + [pl.BlockSpec(memory_space=pltpu.VMEM)] * 2,
        out_specs=(pl.BlockSpec(memory_space=pltpu.HBM),) * 4,
        scratch_shapes=[pltpu.VMEM((own_h, depth), F32), pltpu.VMEM((own_h, depth), F32), dma((4,))],
        compiler_params=pltpu.CompilerParams(vmem_limit_bytes=own_h * depth * 8 + 2 * 1024 * 1024),
    )(*results)
    return tuple(out[None] for out in outs)


def solution(mesh):
    in_specs = (P("section", "expert", None),) * 5 + (P("expert", "section", None),) * 2
    out_specs = (P("section", "expert", None),) * 2 + (P("expert", "section", None),) * 2
    return jax.shard_map(
        per_device, mesh=mesh, in_specs=in_specs, out_specs=out_specs, check_vma=False
    )
```

```python
import functools
import math
import jax
import jax.numpy as jnp
from jax import lax
from jax.experimental import pallas as pl
from jax.experimental.pallas import tpu as pltpu
from jax.sharding import PartitionSpec as P

EPSILON = 1e-06
CHUNKS = 4
ROWS = 16
F32, BF16 = jnp.float32, jnp.bfloat16
NT = (((1,), (1,)), ((), ()))
NN = (((1,), (0,)), ((), ()))
TN = (((0,), (0,)), ((), ()))
FWD, BWD, COT = 0, 1, 2


def mm(a, b, dims):
    return lax.dot_general(a, b, dims, preferred_element_type=F32)


def kernel(
    experts, sections, main, tail,
    xf_hbm, rf_hbm, xb_hbm, rb_hbm, g_hbm, win_hbm, wout_hbm,
    carried, far_next, prev_ref, gin_ref, gout_ref,
    xf_ref, rf_ref, xb_ref, rb_ref, g_ref,
    send, recv, home, back, u_tok, far_tok, far_routes, w_in, w_out, rows_u, rows_g, rows_f, act, slope, hid, side, front,
    tail_rows, part_in, part_out, table, spread, near_sum, far_send, far_part, result,
    loaded, tok_send, tok_recv, route_send, route_recv, near_send, near_recv, home_near, home_far, back_recv,
    cross_send, cross_recv, w_send, w_recv, p_send, p_recv, s_send, s_recv, carry_recv, go,
):
    tokens, depth = xf_hbm.shape
    wide = depth // CHUNKS
    blocks = main // ROWS
    q = ROWS // tail if tail else wide // 256
    thin = wide // q
    own_h = win_hbm.shape[0]
    near = experts // 2
    quarter = experts // 4
    span = near * ROWS
    n_main = experts * main
    me = lax.axis_index("expert")
    sec = lax.axis_index("section")
    half = me // near
    place = lax.rem(me, near)
    column = lax.rem(me, quarter)
    layer = place // quarter
    outward = jnp.where(half == 0, 1 - layer, layer)
    inner = outward == 0
    hub_layer = 1 + half
    my_relay = (2 - half) * quarter + column

    def source(r):
        return (2 - half + r * (1 - 2 * half)) * quarter + column

    def cols(c):
        return pl.ds(pl.multiple_of(c * wide, wide), wide)

    def strip(c, j):
        return pl.ds(pl.multiple_of(c * wide + j * thin, thin), thin)

    loads = [
        pltpu.make_async_copy(src, dst, loaded.at[i])
        for i, (src, dst) in enumerate(
            ((g_hbm, g_ref), (rb_hbm, rb_ref), (rf_hbm, rf_ref), (xb_hbm, xb_ref), (xf_hbm, xf_ref))
        )
    ]
    for load in loads:
        load.start()

    barrier = pltpu.get_barrier_semaphore()

    before, after = lax.rem(sec + sections - 1, sections), lax.rem(sec + 1, sections)
    host = (me == experts - 1) & (sec == 0)
    guest = jnp.logical_not(host)

    @pl.when(inner)
    def _():
        for r in range(2):
            pl.semaphore_signal(barrier, inc=1, device_id={"expert": source(r)})

    @pl.when(guest)
    def _():
        pl.semaphore_signal(barrier, inc=1, device_id={"expert": experts - 1, "section": 0})

    own_rows = pl.ds(pl.multiple_of(sec * own_h, own_h), own_h)

    def routing(which, routes):
        lane_e = lax.broadcasted_iota(jnp.int32, (tokens, near), 1).astype(F32)
        row = lax.broadcasted_iota(jnp.int32, (tokens, tokens), 0)
        col = lax.broadcasted_iota(jnp.int32, (tokens, tokens), 1)
        names = (routes - half * near).astype(F32).astype(BF16)
        columns = mm((row == col).astype(F32).astype(BF16), names, NT)
        named = [columns[:, k : k + 1] for k in range(routes.shape[0])]
        hits = [(i == lane_e).astype(F32) for i in named]
        counts = functools.reduce(jnp.add, hits)
        rank = mm((row > col).astype(F32).astype(BF16), counts.astype(BF16), NN)
        spots = []
        for i, h in zip(named, hits):
            p = jnp.sum(h * rank, axis=1, keepdims=True)
            slot = jnp.full_like(p, -1.0)
            for b in range(blocks):
                low = b * ROWS
                slot = jnp.where((p >= low) & (p < low + ROWS), b * span + i * ROWS + (p - low), slot)
            spots.append((i, p, slot))
        lanes = table.shape[-1]
        lane = lax.broadcasted_iota(jnp.int32, (tokens, lanes), 1).astype(F32)
        for j in range(table.shape[1]):
            hit = jnp.zeros((tokens, lanes), F32)
            for i, p, slot in spots:
                if tail:
                    slot = jnp.where(p >= main, blocks * span + i * ROWS + j * tail + (p - main), slot)
                slot = jnp.where((i >= 0) & (i < near), slot, -1.0)
                hit = jnp.where(lane == slot, 1.0, hit)
            table[which, j] = hit.astype(BF16)

    def normalize(x_ref, which):
        @pl.loop(0, tokens // 16)
        def _(i):
            rows = pl.ds(pl.multiple_of(i * 16, 16), 16)
            x = x_ref[rows, :].astype(F32)
            inv = lax.rsqrt(jnp.mean(x * x, axis=-1, keepdims=True) + EPSILON)
            u_tok[which, rows, :] = (x * inv).astype(BF16)

    def picks(which, j):
        return table[which, j if tail else 0]

    def dispatch(stream, k, c, src):
        which = min(stream, 1) * 3 + k
        total = None
        for j in range(q):
            out = mm(picks(which, j), src[:, strip(c, j)], TN)
            for b in range(blocks):
                send[stream, k, :, c, :, b * wide + j * thin : b * wide + (j + 1) * thin] = (
                    out[b * span : (b + 1) * span].astype(BF16).reshape(near, ROWS, thin)
                )
            if tail:
                rest = out[blocks * span :]
                total = rest if total is None else total + rest
        if tail:
            send[stream, k, :, c, :, blocks * wide :] = total.astype(BF16).reshape(near, ROWS, thin)

    def to_near(stream, k, c, origin):
        pltpu.make_async_copy(
            send.at[stream, k, place, c], recv.at[stream, c, origin], near_recv.at[stream, c]
        ).start()

        @pl.loop(1, near)
        def _(i):
            spot = lax.rem(place + i, near)
            pltpu.make_async_remote_copy(
                src_ref=send.at[stream, k, spot, c],
                dst_ref=recv.at[stream, c, origin],
                send_sem=near_send.at[stream, k],
                recv_sem=near_recv.at[stream, c],
                device_id={"expert": half * near + spot},
            ).start()

    def own_tokens(stream, src):
        @pl.loop(0, CHUNKS)
        def _(c):
            dispatch(stream, 0, c, src)
            to_near(stream, 0, c, me)

    def to_relay(stream, src):
        @pl.loop(0, CHUNKS)
        def _(c):
            pltpu.make_async_remote_copy(
                src_ref=src.at[:, cols(c)], dst_ref=far_tok.at[stream, outward, :, cols(c)],
                send_sem=tok_send.at[stream], recv_sem=tok_recv.at[stream, outward, c],
                device_id={"expert": my_relay},
            ).start()

    def routes_to_relay(micro, src):
        pltpu.make_async_remote_copy(
            src_ref=src, dst_ref=far_routes.at[micro, outward],
            send_sem=route_send.at[micro], recv_sem=route_recv.at[micro, outward],
            device_id={"expert": my_relay},
        ).start()

    def relay_routes(micro):
        @pl.loop(0, 2)
        def _(r):
            mine = far_routes.at[micro, r]
            pltpu.make_async_copy(mine, mine, route_recv.at[micro, r]).wait()
            routing(micro * 3 + 1 + r, far_routes[micro, r])

    def relay(stream, r, low, high):
        @pl.loop(low, high)
        def _(c):
            block = far_tok.at[stream, r, :, cols(c)]
            pltpu.make_async_copy(block, block, tok_recv.at[stream, r, c]).wait()
            dispatch(stream, 1 + r, c, far_tok.at[stream, r])
            to_near(stream, 1 + r, c, source(r))

    def contract(stream, rows_ref, weight, total, low=0, high=CHUNKS):
        if low == 0:
            total[...] = jnp.zeros_like(total)

        @pl.loop(low, high)
        def _(c):
            buf = recv.at[stream, c]
            pltpu.make_async_copy(buf, buf, near_recv.at[stream, c]).wait()
            for b in range(blocks):
                rows_ref[b * experts * ROWS : (b + 1) * experts * ROWS, cols(c)] = buf[
                    :, :, b * wide : (b + 1) * wide
                ].reshape(experts * ROWS, wide)
            if tail:
                for h in range(2):
                    packed = buf[h * near : (h + 1) * near, :, blocks * wide :].reshape(span, thin)
                    for j in range(q):
                        rows_ref[n_main + h * near * tail : n_main + (h + 1) * near * tail, strip(c, j)] = mm(
                            spread[j], packed, NN
                        ).astype(BF16)
            total[...] += mm(rows_ref[:, cols(c)], weight[:, cols(c)], NT)

    def expand(act_rows, weight, slot):
        @pl.loop(0, CHUNKS)
        def _(c):
            buf = home.at[slot, c]
            step = min(512, wide)
            for i in range(wide // step):
                part = pl.ds(pl.multiple_of(c * wide + i * step, step), step)
                out = mm(act_rows[...], weight[:, part], NN).astype(BF16)
                for b in range(blocks):
                    buf[:, :, b * wide + i * step : b * wide + (i + 1) * step] = out[
                        b * experts * ROWS : (b + 1) * experts * ROWS
                    ].reshape(experts, ROWS, step)
                if tail:
                    tail_rows[:, i * step : (i + 1) * step] = out[n_main:]
            if tail:
                for h in range(2):
                    total = None
                    for j in range(q):
                        block = tail_rows[h * near * tail : (h + 1) * near * tail, j * thin : (j + 1) * thin]
                        moved = mm(spread[j], block, TN)
                        total = moved if total is None else total + moved
                    buf[h * near : (h + 1) * near, :, blocks * wide :] = total.astype(BF16).reshape(
                        near, ROWS, thin
                    )
            give_far(slot, c)

    def give_far(slot, c):
        for r in range(2):
            @pl.loop(0, quarter)
            def _(k):
                col = lax.rem(column + k, quarter)
                hub = hub_layer * quarter + col
                block = home.at[slot, c, (2 - half + r * (1 - 2 * half)) * quarter + col]
                there = back.at[slot, c, 1 + r, place]

                @pl.when(hub == me)
                def _():
                    pltpu.make_async_copy(block, there, back_recv.at[slot, c, 1 + r]).start()

                @pl.when(hub != me)
                def _():
                    pltpu.make_async_remote_copy(
                        src_ref=block, dst_ref=there,
                        send_sem=home_far.at[slot], recv_sem=back_recv.at[slot, c, 1 + r],
                        device_id={"expert": hub},
                    ).start()

    def give_near(slot):
        @pl.loop(0, CHUNKS)
        def _(c):
            pltpu.make_async_copy(
                home.at[slot, c, me], back.at[slot, c, 0, place], back_recv.at[slot, c, 0]
            ).start()

            @pl.loop(1, near)
            def _(k):
                peer = half * near + lax.rem(place + k, near)
                pltpu.make_async_remote_copy(
                    src_ref=home.at[slot, c, peer], dst_ref=back.at[slot, c, 0, place],
                    send_sem=home_near.at[slot], recv_sem=back_recv.at[slot, c, 0],
                    device_id={"expert": peer},
                ).start()

    def combine(slot, c, k, out_ref):
        buf = back.at[slot, c, k]
        pltpu.make_async_copy(buf, buf, back_recv.at[slot, c, k]).wait()
        for j in range(q):
            pieces = [
                buf[:, :, b * wide + j * thin : b * wide + (j + 1) * thin].reshape(span, thin) for b in range(blocks)
            ]
            if tail:
                pieces.append(buf[:, :, blocks * wide :].reshape(span, thin))
            out = mm(picks(slot * 3 + k, j), jnp.concatenate(pieces, axis=0), NN)
            out_ref[:, strip(c, j)] = out.astype(out_ref.dtype)

    def cross(slot, c, r):
        combine(slot, c, 1 + r, far_send.at[slot, r])
        pltpu.make_async_remote_copy(
            src_ref=far_send.at[slot, r, :, cols(c)], dst_ref=(far_next if slot == 0 else far_part).at[:, cols(c)],
            send_sem=cross_send.at[slot, r], recv_sem=cross_recv.at[slot, c],
            device_id={"expert": source(r), "section": after if slot == 0 else sec},
        ).start()

    def cross_range(slot, r, low, high):
        @pl.loop(low, high)
        def _(c):
            cross(slot, c, r)

    def own_sum(slot):
        @pl.loop(0, CHUNKS)
        def _(c):
            combine(slot, c, 0, near_sum.at[slot])

    def crossed(slot, c):
        block = (far_next if slot == 0 else far_part).at[:, cols(c)]
        pltpu.make_async_copy(block, block, cross_recv.at[slot, c]).wait()

    def weight_terms(left, right, part):
        step = min(512, depth)

        @pl.loop(0, depth // step)
        def _(j):
            sl = pl.ds(pl.multiple_of(j * step, step), step)
            part[:, sl] = mm(left[...], right[:, sl], TN).astype(BF16)

    def share(i, part, out):
        pltpu.make_async_copy(part.at[own_rows], out.at[sec], p_recv.at[i]).start()

        @pl.loop(1, sections)
        def _(k):
            peer = lax.rem(sec + k, sections)
            pltpu.make_async_remote_copy(
                src_ref=part.at[pl.ds(pl.multiple_of(peer * own_h, own_h), own_h)],
                dst_ref=out.at[sec],
                send_sem=p_send.at[i], recv_sem=p_recv.at[i],
                device_id={"section": peer},
            ).start()

    outer = jnp.logical_not(inner)
    pl.semaphore_wait(barrier, 1 + jnp.where(host, experts * sections - 1, 0))

    @pl.when(host)
    def _():
        @pl.loop(0, experts)
        def _(e):
            @pl.loop(0, sections)
            def _(t):
                @pl.when((e != me) | (t != sec))
                def _():
                    pl.semaphore_signal(go, inc=1, device_id={"expert": e, "section": t})

    routes_to_relay(1, rb_hbm)
    routes_to_relay(0, rf_hbm)

    @pl.when(outer)
    def _():
        to_relay(COT, g_hbm)

    for load in loads[:4]:
        load.wait()
    normalize(xb_ref, 1)

    @pl.when(outer)
    def _():
        to_relay(BWD, u_tok.at[1])

    @pl.when(inner)
    def _():
        to_relay(COT, g_ref)
        to_relay(BWD, u_tok.at[1])

    routing(3, rb_ref[...])

    @pl.when(guest)
    def _():
        pl.semaphore_wait(go, 1)

    own_tokens(COT, g_ref)
    own_tokens(BWD, u_tok.at[1])
    loads[4].wait()
    normalize(xf_ref, 0)
    routing(0, rf_ref[...])

    for i, (src, dst) in enumerate(((win_hbm, w_in), (wout_hbm, w_out))):
        pltpu.make_async_copy(src, dst.at[own_rows], w_recv.at[i]).start()

        @pl.loop(1, sections)
        def _(k):
            pltpu.make_async_remote_copy(
                src_ref=src, dst_ref=dst.at[own_rows],
                send_sem=w_send.at[i], recv_sem=w_recv.at[i],
                device_id={"section": lax.rem(sec + k, sections)},
            ).start()

    if tail:
        shape = (near * tail, span)
        row = lax.broadcasted_iota(jnp.int32, shape, 0).astype(F32)
        col = lax.broadcasted_iota(jnp.int32, shape, 1).astype(F32)
        start = row + jnp.floor((row + 0.5) * (1.0 / tail)) * (ROWS - tail)
        for j in range(q):
            spread[j] = jnp.where(col == start + j * tail, 1.0, 0.0).astype(BF16)

    split = CHUNKS // 2
    last = CHUNKS - 1

    @pl.when(outer)
    def _():
        own_tokens(FWD, u_tok.at[0])

    @pl.when(inner)
    def _():
        to_relay(FWD, u_tok.at[0])
        relay_routes(1)
        relay(COT, 1, 0, CHUNKS)
        relay(BWD, 1, 0, CHUNKS)
        relay_routes(0)
        relay(COT, 0, 0, CHUNKS)
        relay(BWD, 0, 0, split)

    for i, dst in enumerate((w_in, w_out)):
        pltpu.make_async_copy(dst, dst, w_recv.at[i]).wait()

    contract(COT, rows_g, w_out, slope)

    @pl.when(inner)
    def _():
        relay(BWD, 0, split, CHUNKS)
        own_tokens(FWD, u_tok.at[0])

    contract(BWD, rows_u, w_in, act, 0, last)

    @pl.when(outer)
    def _():
        to_relay(FWD, u_tok.at[0])

    contract(BWD, rows_u, w_in, act, last, CHUNKS)
    sigma = jax.nn.sigmoid(act[...])
    hid[...] = (slope[...] * (sigma * (1.0 + act[...] * (1.0 - sigma)))).astype(BF16)
    expand(hid, w_in, 1)
    side[...] = jax.nn.silu(act[...]).astype(BF16)

    @pl.when(inner)
    def _():
        relay(FWD, 1, 0, CHUNKS)
        relay(FWD, 0, 0, last)
        cross_range(1, 0, 0, 1)
        relay(FWD, 0, last, CHUNKS)
        give_near(1)
        cross_range(1, 0, 1, CHUNKS)

    @pl.when(outer)
    def _():
        give_near(1)

    contract(FWD, rows_f, w_in, act)
    front[...] = jax.nn.silu(act[...]).astype(BF16)

    @pl.when(inner)
    def _():
        cross_range(1, 1, 0, split)

    expand(front, w_out, 0)
    give_near(0)

    @pl.when(inner)
    def _():
        cross_range(1, 1, split, CHUNKS)

    weight_terms(hid, rows_u, part_in)
    share(0, part_in, gin_ref)
    weight_terms(side, rows_g, part_out)
    share(1, part_out, gout_ref)
    own_sum(1)

    @pl.when(inner)
    def _():
        @pl.loop(0, CHUNKS)
        def _(c):
            cross(0, c, 1)
            cross(0, c, 0)

    for c in range(CHUNKS):
        crossed(1, c)

    @pl.loop(0, tokens // 16)
    def _(i):
        rows = pl.ds(pl.multiple_of(i * 16, 16), 16)
        x = xb_ref[rows, :].astype(F32)
        total = near_sum[1, rows, :] + far_part[rows, :].astype(F32)
        inv = lax.rsqrt(jnp.mean(x * x, axis=-1, keepdims=True) + EPSILON)
        proj = jnp.mean(total * x, axis=-1, keepdims=True)
        grad = g_ref[rows, :].astype(F32) + inv * total - x * (inv * inv * inv) * proj
        result[rows, :] = grad.astype(BF16)

    to_prev = pltpu.make_async_remote_copy(
        src_ref=result, dst_ref=prev_ref, send_sem=s_send.at[1], recv_sem=s_recv.at[0],
        device_id={"section": lax.rem(sec + sections - 1, sections)},
    )
    to_prev.start()

    @pl.loop(0, CHUNKS)
    def _(c):
        combine(0, c, 0, near_sum.at[0])

        @pl.loop(0, tokens // 16)
        def _(i):
            rows = pl.ds(pl.multiple_of(i * 16, 16), 16)
            near_sum[0, rows, cols(c)] += xf_ref[rows, cols(c)].astype(F32)

        pltpu.make_async_remote_copy(
            src_ref=near_sum.at[0, :, cols(c)], dst_ref=carried.at[:, cols(c)],
            send_sem=s_send.at[0], recv_sem=carry_recv.at[c],
            device_id={"section": after},
        ).start()

    for i, (src, out) in enumerate(((win_hbm, gin_ref), (wout_hbm, gout_ref))):
        pltpu.make_async_copy(out, out, p_recv.at[i]).wait()

        @pl.loop(1, sections)
        def _(k):
            pltpu.make_async_copy(src, src, w_send.at[i]).wait()
            pltpu.make_async_copy(src, src, p_send.at[i]).wait()

    def drain(ref, sem):
        pltpu.make_async_copy(ref, ref, sem).wait()

    for stream in range(3):
        drain(g_ref, tok_send.at[stream])
        drain(send.at[0, 0, pl.ds(0, near - 1)], near_send.at[stream, 0])

    for micro, src in enumerate((rf_ref, rb_ref)):
        drain(src, route_send.at[micro])
    for slot in range(2):
        drain(home.at[0, :, pl.ds(0, near - 1)], home_near.at[slot])

    @pl.when(inner)
    def _():
        for stream in range(3):
            for r in range(2):
                drain(send.at[0, 0, pl.ds(0, near - 1)], near_send.at[stream, 1 + r])
        for slot in range(2):
            drain(home.at[0, :, pl.ds(0, near - 2)], home_far.at[slot])

    @pl.when(jnp.logical_not(inner))
    def _():
        for slot in range(2):
            drain(home.at[0, :, pl.ds(0, near)], home_far.at[slot])

    to_prev.wait()

    for c in range(CHUNKS):
        drain(carried.at[:, cols(c)], carry_recv.at[c])
    for c in range(CHUNKS):
        crossed(0, c)

    drain(carried, s_send.at[0])

    @pl.when(inner)
    def _():
        for slot in range(2):
            for r in range(2):
                drain(far_send.at[slot, r], cross_send.at[slot, r])


def finish(near_ref, far_ref, prev_ref, pin_ref, pout_ref, next_out, prev_out, gin_out, gout_out, total, sum_in, sum_out, sems):
    move = pltpu.make_async_copy(prev_ref, prev_out, sems.at[1])
    move.start()
    for i, (part, whole, out) in enumerate(((pin_ref, sum_in, gin_out), (pout_ref, sum_out, gout_out))):
        step = whole.shape[0] // 4

        @pl.loop(0, 4)
        def _(b):
            @pl.loop(0, step // 16)
            def _(j):
                rows = pl.ds(pl.multiple_of(b * step + j * 16, 16), 16)
                whole[rows, :] = functools.reduce(
                    jnp.add, [part[k, rows, :].astype(F32) for k in range(part.shape[0])]
                )

            block = pl.ds(pl.multiple_of(b * step, step), step)
            pltpu.make_async_copy(whole.at[block], out.at[block], sems.at[2 + i]).start()

    @pl.loop(0, total.shape[0] // 16)
    def _(j):
        rows = pl.ds(pl.multiple_of(j * 16, 16), 16)
        total[rows, :] = (near_ref[rows, :] + far_ref[rows, :].astype(F32)).astype(BF16)

    last = pltpu.make_async_copy(total, next_out, sems.at[0])
    last.start()
    move.wait()
    for i, (whole, out) in enumerate(((sum_in, gin_out), (sum_out, gout_out))):
        pltpu.make_async_copy(whole, out, sems.at[2 + i]).wait()
    last.wait()


def per_device(fwd_states, fwd_routes, bwd_states, bwd_routes, bwd_cot, w_in, w_out):
    experts, sections = lax.axis_size("expert"), lax.axis_size("section")
    _, tokens, depth = fwd_states.shape
    top = fwd_routes.shape[2]
    own_h = w_in.shape[1]
    full_h = own_h * sections
    cap = max(2, (5 * tokens * top + 4 * experts - 1) // (4 * experts))
    main, tail = cap // ROWS * ROWS, cap % ROWS
    tail = next(t for t in (0, 2, 4, 8, 16) if t >= tail)
    main, tail = main + tail // ROWS * ROWS, tail % ROWS
    rows = experts * (main + tail)
    near = experts // 2
    wide = depth // CHUNKS
    q = ROWS // tail if tail else wide // 256
    thin = wide // q
    blocks = main // ROWS
    lanes = blocks * wide + (thin if tail else 0)
    picked = (blocks + (1 if tail else 0)) * near * ROWS
    buffers = [
        pltpu.VMEM((tokens, depth), BF16),
        pltpu.VMEM((top, tokens), jnp.int32),
        pltpu.VMEM((tokens, depth), BF16),
        pltpu.VMEM((top, tokens), jnp.int32),
        pltpu.VMEM((tokens, depth), BF16),
        pltpu.VMEM((3, 3, near, CHUNKS, ROWS, lanes), BF16),
        pltpu.VMEM((3, CHUNKS, experts, ROWS, lanes), BF16),
        pltpu.VMEM((2, CHUNKS, experts, ROWS, lanes), BF16),
        pltpu.VMEM((2, CHUNKS, 3, near, ROWS, lanes), BF16),
        pltpu.VMEM((2, tokens, depth), BF16),
        pltpu.VMEM((3, 2, tokens, depth), BF16),
        pltpu.VMEM((2, 2, top, tokens), jnp.int32),
        pltpu.VMEM((full_h, depth), BF16),
        pltpu.VMEM((full_h, depth), BF16),
        pltpu.VMEM((rows, depth), BF16),
        pltpu.VMEM((rows, depth), BF16),
        pltpu.VMEM((rows, depth), BF16),
        pltpu.VMEM((rows, full_h), F32),
        pltpu.VMEM((rows, full_h), F32),
        pltpu.VMEM((rows, full_h), BF16),
        pltpu.VMEM((rows, full_h), BF16),
        pltpu.VMEM((rows, full_h), BF16),
        pltpu.VMEM((max(ROWS, experts * tail), wide), BF16),
        pltpu.VMEM((full_h, depth), BF16),
        pltpu.VMEM((full_h, depth), BF16),
        pltpu.VMEM((6, q if tail else 1, tokens, picked), BF16),
        pltpu.VMEM((q, max(ROWS, near * tail), near * ROWS), BF16),
        pltpu.VMEM((2, tokens, depth), F32),
        pltpu.VMEM((2, 2, tokens, depth), BF16),
        pltpu.VMEM((tokens, depth), BF16),
        pltpu.VMEM((tokens, depth), BF16),
    ]
    grant = sum(math.prod(b.shape) * jnp.dtype(b.dtype).itemsize for b in buffers) + 3 * 1024 * 1024
    anywhere = pl.BlockSpec(memory_space=pl.ANY)
    dma = pltpu.SemaphoreType.DMA
    states = jax.ShapeDtypeStruct((tokens, depth), BF16)
    parts = jax.ShapeDtypeStruct((sections, own_h, depth), BF16)
    grads = jax.ShapeDtypeStruct((own_h, depth), F32)
    operands = (fwd_states[0], fwd_routes[0].T, bwd_states[0], bwd_routes[0].T, bwd_cot[0], w_in[0], w_out[0])
    results = pl.pallas_call(
        functools.partial(kernel, experts, sections, main, tail),
        out_shape=(jax.ShapeDtypeStruct((tokens, depth), F32), states, states, parts, parts),
        in_specs=[pl.BlockSpec(memory_space=pltpu.HBM)] * 7,
        out_specs=(anywhere,) * 5,
        scratch_shapes=[
            *buffers,
            dma((5,)), dma((3,)), dma((3, 2, CHUNKS)), dma((2,)), dma((2, 2)), dma((3, 3)), dma((3, CHUNKS)),
            dma((2,)), dma((2,)), dma((2, CHUNKS, 3)), dma((2, 2)), dma((2, CHUNKS)),
            dma((2,)), dma((2,)), dma((2,)), dma((2,)), dma((2,)), dma((1,)), dma((CHUNKS,)), pltpu.SemaphoreType.REGULAR,
        ],
        compiler_params=pltpu.CompilerParams(
            collective_id=0, has_side_effects=True, vmem_limit_bytes=grant
        ),
    )(*(pltpu.with_memory_space_constraint(v, pltpu.HBM) for v in operands))
    local = pl.BlockSpec(memory_space=pltpu.VMEM)
    outs = pl.pallas_call(
        finish,
        out_shape=(states, states, grads, grads),
        in_specs=[local, local, anywhere, local, local],
        out_specs=(pl.BlockSpec(memory_space=pltpu.HBM),) * 4,
        scratch_shapes=[
            pltpu.VMEM((tokens, depth), BF16), pltpu.VMEM((own_h, depth), F32), pltpu.VMEM((own_h, depth), F32), dma((4,)),
        ],
        compiler_params=pltpu.CompilerParams(vmem_limit_bytes=(8 * own_h + 2 * tokens) * depth + 2 * 1024 * 1024),
    )(*results)
    return tuple(out[None] for out in outs)


def solution(mesh):
    in_specs = (P("section", "expert", None),) * 5 + (P("expert", "section", None),) * 2
    out_specs = (P("section", "expert", None),) * 2 + (P("expert", "section", None),) * 2
    return jax.shard_map(
        per_device, mesh=mesh, in_specs=in_specs, out_specs=out_specs, check_vma=False
    )
```
